32 devices in a mesh: dp: 8 (over z, y), tensor: 4 (over x, core).
Axes of the slice: x: 2, y: 2, z: 4, core: 2. Of those that a mesh axis runs over, the one named last changes fastest.
Arguments:
- frames: bfloat16 [8, 1024, 768], P('dp'), may hold values from -6 to 6
- frame_mask: int32 [8, 1024], P('dp'), may hold values from 0 to 1, as said below
- mask_embedding: float32 [768], replicated, may hold values from -6 to 6
- query_weight: bfloat16 [768, 768], P(None, 'tensor'), may hold values from -0.21875 to 0.21875
- query_bias: float32 [768], P('tensor'), may hold values from -3 to 3
- key_weight: bfloat16 [768, 768], P(None, 'tensor'), may hold values from -0.21875 to 0.21875
- value_weight: bfloat16 [768, 768], P(None, 'tensor'), may hold values from -0.21875 to 0.21875
- value_bias: float32 [768], P('tensor'), may hold values from -3 to 3
- out_weight: bfloat16 [768, 768], P('tensor'), may hold values from -0.625 to 0.625
- out_bias: float32 [768], replicated, may hold values from -3 to 3
- norm1_gain: float32 [768], replicated, may hold values from 0.5 to 1.5
- norm1_shift: float32 [768], replicated, may hold values from -3 to 3
- up_weight: bfloat16 [768, 3072], P(None, 'tensor'), may hold values from -0.21875 to 0.21875
- up_bias: float32 [3072], P('tensor'), may hold values from -3 to 3
- down_weight: bfloat16 [3072, 768], P('tensor'), may hold values from -0.109375 to 0.109375
- down_bias: float32 [768], replicated, may hold values from -3 to 3
- norm2_gain: float32 [768], replicated, may hold values from 0.5 to 1.5
- norm2_shift: float32 [768], replicated, may hold values from -3 to 3
- cotangent: bfloat16 [8, 1024, 768], P('dp'), may hold values from -6 to 6
Outputs:
- output: bfloat16 [8, 1024, 768], P('dp')
- frames_grad: bfloat16 [8, 1024, 768], P('dp')
- mask_embedding_grad: float32 [768], replicated
- query_weight_grad: float32 [768, 768], P(None, 'tensor')
- query_bias_grad: float32 [768], P('tensor')
- key_weight_grad: float32 [768, 768], P(None, 'tensor')
- value_weight_grad: float32 [768, 768], P(None, 'tensor')
- value_bias_grad: float32 [768], P('tensor')
- out_weight_grad: float32 [768, 768], P('tensor')
- out_bias_grad: float32 [768], replicated
- norm1_gain_grad: float32 [768], replicated
- norm1_shift_grad: float32 [768], replicated
- up_weight_grad: float32 [768, 3072], P(None, 'tensor')
- up_bias_grad: float32 [3072], P('tensor')
- down_weight_grad: float32 [3072, 768], P('tensor')
- down_bias_grad: float32 [768], replicated
- norm2_gain_grad: float32 [768], replicated
- norm2_shift_grad: float32 [768], replicated
The draws below stay inside these ranges and needn't reach their ends.
Inputs may be any that keep to these rules, and one draw needn't show every extreme that they name: `frame_mask`: 1 marks a frame inside one of 68 spans of 10 frames whose starts are drawn for each clip; spans may intersect.
All inputs are finite; a program needn't handle non-finite values.
Results may differ from the reference program's by a relative error of at most 0.017.
Values sent between devices are 32-bit elements; how exact they have to be, the bound alone decides.
No kernel may reach another device: no remote copies, remote signals or barrier semaphores. Data moves between devices by JAX's collectives and lax.ppermute only.
A program may use at most 128 MiB of HBM per device.

```python
import math
import jax
import jax.numpy as jnp
from jax import lax

D = 768
HEADS = 12
HEAD = 64
FF = 3072
LEN = 1024
MSPAN = 10
SPANS = 68
CLIPS = 8


def draw_frame_mask(key, part):
    starts = jax.random.randint(key, (CLIPS, SPANS), 0, LEN - MSPAN + 1)
    position = jnp.arange(LEN)
    inside = (position[None, None, :] >= starts[:, :, None]) & (position[None, None, :] < starts[:, :, None] + MSPAN)
    return jnp.any(inside, axis=1).astype(jnp.int32)


def shard_levels(stream_key, shape, split, low, largest):
    def one(dim, blocks):
        draws = jax.random.uniform(jax.random.fold_in(jax.random.fold_in(stream_key, 6), dim), (blocks,), jnp.float32, low / len(split), largest / len(split))
        return jnp.repeat(jnp.exp(draws), shape[dim] // blocks).reshape((-1,) + (1,) * (len(shape) - dim - 1))

    gain = one(*split[0])
    for cut in split[1:]:
        gain = gain * one(*cut)
    return gain


def noise(own_key, extent, deviation, limit, shards=(), kind=jnp.bfloat16):
    values = jax.random.normal(own_key, extent, jnp.float32) * deviation
    if len(shards) > 0:
        values = shard_levels(own_key, extent, shards, -0.22, 0.18) * values
    return jnp.clip(values, min=-limit, max=limit).astype(kind)


def setup_inputs(seed: int = 0) -> dict:
    seeds = jax.random.split(jax.random.key(seed), 20)
    frames = noise(seeds[0], (CLIPS, LEN, D), 1.0, 6.0, ((0, 8),))
    frame_mask = draw_frame_mask(jax.random.fold_in(seeds[19], 71), 0)
    mask_embedding = noise(seeds[2], (D,), 1.0, 6.0, (), jnp.float32)
    query_weight = noise(seeds[3], (D, D), D ** -0.5, 0.21875, ((1, 4),))
    query_bias = noise(seeds[4], (D,), 0.5, 3.0, ((0, 4),), jnp.float32)
    key_weight = noise(seeds[5], (D, D), D ** -0.5, 0.21875, ((1, 4),))
    value_weight = noise(seeds[6], (D, D), D ** -0.5, 0.21875, ((1, 4),))
    value_bias = noise(seeds[7], (D,), 0.5, 3.0, ((0, 4),), jnp.float32)
    out_weight = noise(seeds[8], (D, D), (D // 8) ** -0.5, 0.625, ((0, 4),))
    out_bias = noise(seeds[9], (D,), 0.5, 3.0, (), jnp.float32)
    norm1_gain = jnp.clip(1.0 + 0.1 * jax.random.normal(seeds[10], (D,), jnp.float32), 0.5, 1.5)
    norm1_shift = noise(seeds[11], (D,), 0.5, 3.0, (), jnp.float32)
    up_weight = noise(seeds[12], (D, FF), D ** -0.5, 0.21875, ((1, 4),))
    up_bias = noise(seeds[13], (FF,), 0.5, 3.0, ((0, 4),), jnp.float32)
    down_weight = noise(seeds[14], (FF, D), FF ** -0.5, 0.109375, ((0, 4),))
    down_bias = noise(seeds[15], (D,), 0.5, 3.0, (), jnp.float32)
    norm2_gain = jnp.clip(1.0 + 0.1 * jax.random.normal(seeds[16], (D,), jnp.float32), 0.5, 1.5)
    norm2_shift = noise(seeds[17], (D,), 0.5, 3.0, (), jnp.float32)
    cotangent = noise(seeds[18], (CLIPS, LEN, D), 1.0, 6.0, ((0, 8),))
    return {"frames": frames, "frame_mask": frame_mask, "mask_embedding": mask_embedding, "query_weight": query_weight, "query_bias": query_bias, "key_weight": key_weight, "value_weight": value_weight, "value_bias": value_bias, "out_weight": out_weight, "out_bias": out_bias, "norm1_gain": norm1_gain, "norm1_shift": norm1_shift, "up_weight": up_weight, "up_bias": up_bias, "down_weight": down_weight, "down_bias": down_bias, "norm2_gain": norm2_gain, "norm2_shift": norm2_shift, "cotangent": cotangent}


@jax.custom_vjp
def low(v):
    return lax.optimization_barrier(v.astype(jnp.bfloat16)).astype(jnp.float32)

@jax.custom_vjp
def low_back(v):
    return v

def low_keep(v):
    return (low(v), None)

def low_pass(kept, grad):
    return (grad,)

def back_keep(v):
    return (v, None)

def back_low(kept, grad):
    return (low(grad),)
low.defvjp(low_keep, low_pass)
low_back.defvjp(back_keep, back_low)

def dense_high(left, right):
    return jnp.dot(left, right, precision=lax.Precision.HIGHEST)

def layer_norm(values, gain_vec, shift_vec):
    centered = values - lax.optimization_barrier(jnp.mean(values, -1, keepdims=True))
    variance = lax.optimization_barrier(jnp.mean(centered * centered, -1, keepdims=True))
    return centered * lax.rsqrt(variance + 1e-05) * gain_vec + shift_vec

def forward(params, frames_all, mask_all):
    mask_embedding, query_weight, query_bias, key_weight, value_weight, value_bias, out_weight, out_bias, norm1_gain, norm1_shift, up_weight, up_bias, down_weight, down_bias, norm2_gain, norm2_shift = params
    score_scale = 1.0 / math.sqrt(HEAD)

    def one_clip(pair):
        frames_clip, mask_clip = pair
        masked_rows = mask_clip[:, None]
        masked_in = frames_clip * (1.0 - masked_rows) + masked_rows * mask_embedding
        masked_low = low(masked_in)
        query = low(low_back(dense_high(masked_low, query_weight) + query_bias))
        keys = low(low_back(dense_high(masked_low, key_weight)))
        values = low(low_back(dense_high(masked_low, value_weight) + value_bias))
        query_heads = query.reshape(LEN, HEADS, HEAD)
        key_heads = keys.reshape(LEN, HEADS, HEAD)
        value_heads = values.reshape(LEN, HEADS, HEAD)
        scores = low_back(jnp.einsum('qhd,khd->hqk', query_heads, key_heads, precision=lax.Precision.HIGHEST) * score_scale)
        attn_low = low(jax.nn.softmax(scores, axis=-1))
        context = jnp.einsum('hqk,khd->qhd', attn_low, value_heads, precision=lax.Precision.HIGHEST).reshape(LEN, D)
        context = low(low_back(context))
        attended = low_back(dense_high(context, out_weight)) + out_bias
        hidden_one = layer_norm(masked_in + attended, norm1_gain, norm1_shift)
        ffn_in = low(hidden_one)
        pre_act = low_back(dense_high(ffn_in, up_weight) + up_bias)
        activ = low(jax.nn.gelu(pre_act, approximate=False))
        ffn_out = low_back(dense_high(activ, down_weight)) + down_bias
        return layer_norm(hidden_one + ffn_out, norm2_gain, norm2_shift)
    return lax.map(jax.checkpoint(one_clip), (frames_all, mask_all))

def reference(frames, frame_mask, mask_embedding, query_weight, query_bias, key_weight, value_weight, value_bias, out_weight, out_bias, norm1_gain, norm1_shift, up_weight, up_bias, down_weight, down_bias, norm2_gain, norm2_shift, cotangent):
    params = tuple((item.astype(jnp.float32) for item in (mask_embedding, query_weight, query_bias, key_weight, value_weight, value_bias, out_weight, out_bias, norm1_gain, norm1_shift, up_weight, up_bias, down_weight, down_bias, norm2_gain, norm2_shift)))
    frames_full = frames.astype(jnp.float32)
    mask_full = frame_mask.astype(jnp.float32)
    output, pullback = jax.vjp(lambda prm, fts: forward(prm, fts, mask_full), params, frames_full)
    grads, frames_grad = pullback(cotangent.astype(jnp.float32))
    return (output.astype(jnp.bfloat16), frames_grad.astype(jnp.bfloat16), grads[0], grads[1], grads[2], grads[3], grads[4], grads[5], grads[6], grads[7], grads[8], grads[9], grads[10], grads[11], grads[12], grads[13], grads[14], grads[15])
```

```python
import math

import jax
import jax.numpy as jnp
from jax import lax
from jax.sharding import PartitionSpec as P

HEAD = 64
AXES = ("dp", "tensor")
STEPS = 2


def local_dot(left, right):
    return jnp.dot(left, right, preferred_element_type=jnp.float32)


def dot_rows(left, right):
    return lax.dot_general(
        left, right, (((0,), (0,)), ((), ())), preferred_element_type=jnp.float32
    )


def dot_trans(left, right):
    return lax.dot_general(
        left, right, (((1,), (1,)), ((), ())), preferred_element_type=jnp.float32
    )


def normalize(values):
    centered = values - jnp.mean(values, -1, keepdims=True)
    inverse = lax.rsqrt(jnp.mean(centered * centered, -1, keepdims=True) + 1e-05)
    return (centered * inverse, inverse)


def norm_backward(grad_normed, normed, inverse):
    return inverse * (
        grad_normed
        - jnp.mean(grad_normed, -1, keepdims=True)
        - normed * jnp.mean(grad_normed * normed, -1, keepdims=True)
    )


class Swaps:
    def __init__(self, mesh):
        self.dp = mesh.shape["dp"]
        self.tensor = mesh.shape["tensor"]
        index = lax.axis_index("dp")
        self.masks = [1 << bit for bit in range(self.dp.bit_length() - 1)]
        self.coords = [(index >> bit) & 1 for bit in range(len(self.masks))]
        if len(self.masks) >= 3:
            self.masks[2] = 6
            self.coords[1] = self.coords[1] ^ self.coords[2]
        self.core = lax.axis_index("tensor") % 2

    def move(self, value, target):
        pairs = []
        for row in range(self.dp):
            for column in range(self.tensor):
                to_row, to_column = target(row, column)
                pairs.append((row * self.tensor + column, to_row * self.tensor + to_column))
        return lax.ppermute(value, AXES, pairs)

    def over_core(self, value):
        return self.move(value, lambda row, column: (row, column ^ 1))

    def over_chip(self, value):
        return self.move(value, lambda row, column: (row, column ^ 2))

    def over_dp(self, value, even, odd):
        masks = self.masks
        return self.move(
            value, lambda row, column: (row ^ masks[odd if column % 2 else even], column)
        )

    def plan(self):
        steps = list(range(len(self.masks)))
        result = []
        for even, odd in zip(steps, steps[-1:] + steps[:-1]):
            coord = jnp.where(self.core == 0, self.coords[even], self.coords[odd])
            result.append((even, odd, coord))
        return result


class Order:
    def __init__(self):
        self.last = ()

    def begin(self, *arrays):
        arrays, _ = lax.optimization_barrier((arrays, self.last))
        return arrays[0] if len(arrays) == 1 else arrays

    def end(self, *arrays):
        self.last = arrays
        return arrays[0] if len(arrays) == 1 else arrays


class Total:
    def __init__(self, swaps, order, value):
        self.swaps, self.order, self.plan = swaps, order, swaps.plan()
        self.queue = [self.first] + [self.halve] * (len(self.plan) - 2)
        self.queue += [self.exchange, self.settle] + [self.double] * (len(self.plan) - 1)
        self.keep, self.got, self.at = value, None, 0
        self.advance()

    def advance(self, count=1):
        for _ in range(count):
            if self.queue:
                self.queue.pop(0)()

    def send(self, value):
        even, odd, _ = self.plan[self.at]
        self.got = self.swaps.over_dp(value, even, odd)

    def first(self):
        coord = self.plan[0][2]
        rows = self.keep.shape[0] // 2
        value = self.order.begin(self.keep)
        self.send(self.order.end(pick(value, 1 - coord, rows)))
        self.keep = pick(value, coord, rows)

    def halve(self):
        self.at += 1
        coord = self.plan[self.at][2]
        rows = self.keep.shape[0] // 2
        keep, got = self.order.begin(self.keep, self.got)
        send = pick(keep, 1 - coord, rows) + pick(got, 1 - coord, rows)
        self.keep = pick(keep, coord, rows) + pick(got, coord, rows)
        self.order.end(send, self.keep)
        self.send(send)

    def exchange(self):
        self.at += 1
        keep, got = self.order.begin(self.keep, self.got)
        self.keep = self.order.end(keep + got)
        self.send(self.keep)

    def settle(self):
        keep, got = self.order.begin(self.keep, self.got)
        self.keep = self.order.end(keep + got)
        self.at -= 1
        self.send(self.keep)

    def double(self):
        first = self.plan[self.at][2] == 0
        keep, got = self.order.begin(self.keep, self.got)
        self.keep = self.order.end(
            jnp.concatenate([jnp.where(first, keep, got), jnp.where(first, got, keep)], 0)
        )
        self.at -= 1
        if self.at >= 0:
            self.send(self.keep)

    def finish(self):
        self.advance(len(self.queue))
        return self.keep


def pick(block, part, rows):
    return lax.dynamic_slice_in_dim(block, part * rows, rows, 0)


def widen(array):
    return array.astype(jnp.float32) * 2.0


def narrow(array):
    return (array * 0.5).astype(jnp.bfloat16)


def shards(
    mesh,
    frames,
    frame_mask,
    mask_embedding,
    query_weight,
    query_bias,
    key_weight,
    value_weight,
    value_bias,
    out_weight,
    out_bias,
    norm1_gain,
    norm1_shift,
    up_weight,
    up_bias,
    down_weight,
    down_bias,
    norm2_gain,
    norm2_shift,
    cotangent,
):
    swaps = Swaps(mesh)
    order = Order()
    clip_count, length, model_width = frames.shape
    token_rows = clip_count * length
    local_width = query_weight.shape[1]
    heads_here = local_width // HEAD
    score_scale = 1.0 / math.sqrt(HEAD)
    head_shape = (clip_count, length, heads_here, HEAD)
    own_rows = token_rows // 2
    step_rows = own_rows // STEPS
    core = swaps.core
    tensor_index = lax.axis_index("tensor")

    def own_first(array):
        view = array.reshape((2, own_rows) + array.shape[1:])
        return jnp.where(core == 0, view, view[::-1]).reshape(array.shape)

    def step(array, k):
        return array[k * step_rows : (k + 1) * step_rows]

    out_all = lax.all_gather(widen(out_weight), "tensor", tiled=True)
    up_pair = swaps.over_core(widen(up_weight))
    down_pair = swaps.over_core(widen(down_weight))
    up_bias_pair = swaps.over_core(up_bias.reshape(1, -1))[0]

    masked_rows = own_first(frame_mask.reshape(token_rows, 1)).astype(jnp.float32)
    masked_in = (
        own_first(frames.reshape(token_rows, model_width)).astype(jnp.float32)
        * (1.0 - masked_rows)
        + masked_rows * mask_embedding
    )
    grad_out = pick(cotangent.reshape(token_rows, model_width), core, own_rows).astype(jnp.float32)
    masked_low = masked_in.astype(jnp.bfloat16)
    query = (local_dot(masked_low, query_weight) + query_bias).astype(jnp.bfloat16)
    keys = local_dot(masked_low, key_weight).astype(jnp.bfloat16)
    values = (local_dot(masked_low, value_weight) + value_bias).astype(jnp.bfloat16)
    query_heads = query.reshape(head_shape)
    key_heads = keys.reshape(head_shape)
    value_heads = values.reshape(head_shape)
    scores = (
        jnp.einsum("cqhd,ckhd->chqk", query_heads, key_heads, preferred_element_type=jnp.float32)
        * score_scale
    )
    row_max = jnp.max(scores, -1, keepdims=True)
    expo = jnp.exp(scores - row_max)
    totals = jnp.sum(expo, -1, keepdims=True)
    log_sum = row_max + jnp.log(totals)
    attn_low = (expo / totals).astype(jnp.bfloat16)
    context = jnp.einsum(
        "chqk,ckhd->cqhd", attn_low, value_heads, preferred_element_type=jnp.float32
    )
    context = context.reshape(token_rows, local_width).astype(jnp.bfloat16)

    context_pair = swaps.over_core(widen(context[own_rows:]))
    chip_wide = jnp.concatenate([widen(context[:own_rows]), context_pair], 1)
    other_wide = [swaps.over_chip(step(chip_wide, k)) for k in range(STEPS)]
    context_chip = narrow(order.end(chip_wide))
    out_all = narrow(out_all)
    out_parts = [pick(out_all, tensor_index ^ mask, local_width) for mask in (0, 1, 2, 3)]
    out_chip = jnp.concatenate(out_parts[:2], 0)
    out_other = jnp.concatenate(out_parts[2:], 0)
    up_chip = jnp.concatenate([up_weight, narrow(up_pair)], 1)
    up_bias_chip = jnp.concatenate([up_bias, up_bias_pair])
    down_chip = jnp.concatenate([down_weight, narrow(down_pair)], 0)
    units_here = up_weight.shape[1]

    normed_one, inverse_one, ffn_in, activ, slope = [], [], [], [], []
    hidden_one, ffn_part, ffn_got = [], [], []
    for k in range(STEPS):
        rows, wide = order.begin(step(context_chip, k), other_wide[k])
        attended = local_dot(rows, out_chip) + local_dot(narrow(wide), out_other)
        normed, inverse = normalize(step(masked_in, k) + attended + out_bias)
        hidden = normed * norm1_gain + norm1_shift
        low = hidden.astype(jnp.bfloat16)
        pre_act = local_dot(low, up_chip) + up_bias_chip
        normal_cdf = 0.5 * (1.0 + lax.erf(pre_act / math.sqrt(2.0)))
        normal_pdf = jnp.exp(-0.5 * pre_act * pre_act) / math.sqrt(2.0 * math.pi)
        units = (pre_act * normal_cdf).astype(jnp.bfloat16)
        part = order.end(local_dot(units, down_chip))
        ffn_part.append(part)
        ffn_got.append(swaps.over_chip(part))
        normed_one.append(normed)
        inverse_one.append(inverse)
        hidden_one.append(hidden)
        ffn_in.append(low)
        activ.append(units)
        slope.append(normal_cdf + pre_act * normal_pdf)

    output, grad_h2, grad_h2_low, grad_pre, one_part, one_got = [], [], [], [], [], []
    gain_two, shift_two, bias_down, bias_up = [], [], [], []
    for k in range(STEPS):
        part, got = order.begin(ffn_part[k], ffn_got[k])
        normed, inverse = normalize(hidden_one[k] + (part + got) + down_bias)
        output.append(normed)
        grad = step(grad_out, k)
        gain_two.append(jnp.sum(grad * normed, 0))
        shift_two.append(jnp.sum(grad, 0))
        grad_two = norm_backward(grad * norm2_gain, normed, inverse)
        bias_down.append(jnp.sum(grad_two, 0))
        low = grad_two.astype(jnp.bfloat16)
        units = (dot_trans(low, down_chip) * slope[k]).astype(jnp.bfloat16)
        bias_up.append(jnp.sum(units.astype(jnp.float32), 0))
        part = order.end(dot_trans(units, up_chip))
        one_part.append(part)
        one_got.append(swaps.over_chip(part))
        grad_h2.append(grad_two)
        grad_h2_low.append(low)
        grad_pre.append(units)

    activ = jnp.concatenate(activ, 0)
    grad_h2_low = jnp.concatenate(grad_h2_low, 0)
    activ, grad_h2_low = order.begin(activ, grad_h2_low)
    down_send = order.end(dot_rows(activ[:, units_here:], grad_h2_low))
    down_got = swaps.over_core(down_send)
    activ, grad_h2_low = order.begin(activ, grad_h2_low)
    down_keep = order.end(dot_rows(activ[:, :units_here], grad_h2_low))
    ffn_in = jnp.concatenate(ffn_in, 0)
    grad_pre = jnp.concatenate(grad_pre, 0)
    ffn_in, grad_pre = order.begin(ffn_in, grad_pre)
    up_send = order.end(dot_rows(ffn_in, grad_pre[:, units_here:]))
    up_got = swaps.over_core(up_send)
    down_keep, down_got = order.begin(down_keep, down_got)
    down_total = Total(swaps, order, order.end(down_keep + down_got))
    ffn_in, grad_pre = order.begin(ffn_in, grad_pre)
    up_keep = order.end(dot_rows(ffn_in, grad_pre[:, :units_here]))
    up_keep, up_got = order.begin(up_keep, up_got)
    up_total = Total(swaps, order, order.end(up_keep + up_got))

    gain_one, shift_one, bias_out, grad_h1, grad_h1_low, wide_context = [], [], [], [], [], []
    context_grads = []
    for k in range(STEPS):
        part, got = order.begin(one_part[k], one_got[k])
        grad_one = grad_h2[k] + (part + got)
        gain_one.append(jnp.sum(grad_one * normed_one[k], 0))
        shift_one.append(jnp.sum(grad_one, 0))
        grad = norm_backward(grad_one * norm1_gain, normed_one[k], inverse_one[k])
        bias_out.append(jnp.sum(grad, 0))
        low = grad.astype(jnp.bfloat16)
        grad_h1.append(grad)
        grad_h1_low.append(low)
        wide_context.append(widen(dot_trans(low, out_parts[1]).astype(jnp.bfloat16)))
        context_grads.append(dot_trans(low, out_parts[0]).astype(jnp.bfloat16))
        order.end(wide_context[-1], context_grads[-1])
        if k == STEPS // 2 - 1:
            down_total.advance()
    got = swaps.over_core(jnp.concatenate(wide_context, 0))
    down_total.advance()
    up_total.advance()
    grad_context = jnp.concatenate(context_grads + [narrow(got)], 0).reshape(head_shape)
    grad_h1_low = jnp.concatenate(grad_h1_low, 0)

    grad_context, scale_sum = order.begin(grad_context, log_sum)
    scores_again = (
        jnp.einsum("cqhd,ckhd->chqk", query_heads, key_heads, preferred_element_type=jnp.float32)
        * score_scale
    )
    attn_again = jnp.exp(scores_again - scale_sum)
    attn_again_low = attn_again.astype(jnp.bfloat16)
    grad_values = jnp.einsum(
        "chqk,cqhd->ckhd", attn_again_low, grad_context, preferred_element_type=jnp.float32
    )
    grad_values = grad_values.astype(jnp.bfloat16).reshape(token_rows, local_width)
    grad_attn = jnp.einsum(
        "cqhd,ckhd->chqk", grad_context, value_heads, preferred_element_type=jnp.float32
    )
    grad_scores = (
        attn_again * (grad_attn - jnp.sum(attn_again * grad_attn, -1, keepdims=True))
    ).astype(jnp.bfloat16)
    order.end(grad_scores, grad_values)
    down_total.advance()
    up_total.advance()
    grad_scores = order.begin(grad_scores)
    grad_query = (
        jnp.einsum("chqk,ckhd->cqhd", grad_scores, key_heads, preferred_element_type=jnp.float32)
        * score_scale
    )
    grad_query = grad_query.astype(jnp.bfloat16).reshape(token_rows, local_width)
    grad_keys = (
        jnp.einsum("chqk,cqhd->ckhd", grad_scores, query_heads, preferred_element_type=jnp.float32)
        * score_scale
    )
    grad_keys = grad_keys.astype(jnp.bfloat16).reshape(token_rows, local_width)
    three = order.end(jnp.concatenate([grad_query, grad_keys, grad_values], 1))
    attn_weight = jnp.concatenate([query_weight, key_weight, value_weight], 1)

    three = order.begin(three)
    terms_send = order.end(dot_trans(three[own_rows:], attn_weight))
    terms_got = swaps.over_core(terms_send)
    three = order.begin(three)
    terms_keep = order.end(dot_trans(three[:own_rows], attn_weight))
    chip_terms, chip_got = [], []
    for k in range(2):
        rows = own_rows // 2
        part, got = order.begin(
            terms_keep[k * rows : (k + 1) * rows], terms_got[k * rows : (k + 1) * rows]
        )
        chip_terms.append(order.end(part + got))
        chip_got.append(swaps.over_chip(chip_terms[-1]))
    three = order.begin(three)
    attn_total = Total(swaps, order, order.end(dot_rows(masked_low, three)))
    grad_h1_low, context_chip = order.begin(grad_h1_low, context_chip)
    out_send = order.end(dot_rows(context_chip[:, local_width:], grad_h1_low))
    out_got = swaps.over_core(out_send)
    out_keep = order.end(dot_rows(context_chip[:, :local_width], grad_h1_low))
    down_total.advance()
    up_total.advance()
    out_keep, out_got = order.begin(out_keep, out_got)
    out_total = Total(swaps, order, order.end(out_keep + out_got))
    attn_total.advance()
    down_total.advance()
    up_total.advance()

    frames_part, mask_sums = [], []
    unmasked = 1.0 - masked_rows
    for k in range(2):
        rows = own_rows // 2
        part, got = order.begin(chip_terms[k], chip_got[k])
        grad_in = jnp.concatenate(grad_h1, 0)[k * rows : (k + 1) * rows] + (part + got)
        mask_sums.append(jnp.sum(grad_in * masked_rows[k * rows : (k + 1) * rows], 0))
        frames_part.append(order.end(grad_in))
        down_total.advance()
        up_total.advance()
        attn_total.advance()
        out_total.advance()
    frames_part = jnp.concatenate(frames_part, 0)
    frames_got = swaps.over_core(frames_part)
    output = jnp.concatenate(output, 0)
    output_got = swaps.over_core(output)

    shared = (
        sum(mask_sums),
        sum(bias_out),
        sum(gain_one),
        sum(shift_one),
        sum(bias_down),
        sum(gain_two),
        sum(shift_two),
    )
    own_bias_up = sum(bias_up)
    pair = jnp.concatenate(shared + (own_bias_up[units_here:],))[None]
    mine = jnp.concatenate(shared + (own_bias_up[:units_here],))[None]
    packed = mine + swaps.over_core(pair)
    packed = jnp.concatenate(
        [
            packed,
            jnp.sum(grad_query.astype(jnp.float32), 0)[None],
            jnp.sum(grad_values.astype(jnp.float32), 0)[None],
        ],
        1,
    )
    for link in range(len(swaps.masks)):
        packed = packed + swaps.over_dp(packed, link, link)
    pieces = []
    start = 0
    for width in [model_width] * 7 + [units_here] + [local_width] * 2:
        pieces.append(packed[0, start : start + width])
        start += width
    (
        mask_embedding_grad,
        out_bias_grad,
        norm1_gain_grad,
        norm1_shift_grad,
        down_bias_grad,
        norm2_gain_grad,
        norm2_shift_grad,
        up_bias_grad,
        query_bias_grad,
        value_bias_grad,
    ) = pieces
    down_weight_grad = down_total.finish()
    up_weight_grad = up_total.finish()
    for _ in range(4):
        attn_total.advance()
        out_total.advance()
    attn_weight_grad = attn_total.finish()
    out_weight_grad = out_total.finish()
    query_weight_grad = attn_weight_grad[:, :local_width]
    key_weight_grad = attn_weight_grad[:, local_width : 2 * local_width]
    value_weight_grad = attn_weight_grad[:, 2 * local_width :]

    def in_place(own, got):
        whole = jnp.stack([jnp.where(core == 0, own, got), jnp.where(core == 0, got, own)])
        return whole.reshape(token_rows, model_width)

    frames_grad = in_place(frames_part, frames_got) * (
        1.0 - frame_mask.reshape(token_rows, 1).astype(jnp.float32)
    )
    output = in_place(output, output_got) * norm2_gain + norm2_shift
    return (
        output.astype(jnp.bfloat16).reshape(frames.shape),
        frames_grad.astype(jnp.bfloat16).reshape(frames.shape),
        mask_embedding_grad,
        query_weight_grad,
        query_bias_grad,
        key_weight_grad,
        value_weight_grad,
        value_bias_grad,
        out_weight_grad,
        out_bias_grad,
        norm1_gain_grad,
        norm1_shift_grad,
        up_weight_grad,
        up_bias_grad,
        down_weight_grad,
        down_bias_grad,
        norm2_gain_grad,
        norm2_shift_grad,
    )


def solution(mesh):
    rows, columns, whole, vector = P("dp"), P(None, "tensor"), P(), P("tensor")
    return jax.shard_map(
        lambda *arrays: shards(mesh, *arrays),
        mesh=mesh,
        in_specs=(
            P("dp", None, None),
            P("dp", None),
            whole,
            columns,
            vector,
            columns,
            columns,
            vector,
            P("tensor", None),
            whole,
            whole,
            whole,
            columns,
            vector,
            P("tensor", None),
            whole,
            whole,
            whole,
            P("dp", None, None),
        ),
        out_specs=(
            P("dp", None, None),
            P("dp", None, None),
            whole,
            columns,
            vector,
            columns,
            columns,
            vector,
            P("tensor", None),
            whole,
            whole,
            whole,
            columns,
            vector,
            P("tensor", None),
            whole,
            whole,
            whole,
        ),
        check_vma=False,
    )
```

```python
import math

import jax
import jax.numpy as jnp
from jax import lax
from jax.experimental import pallas as pl
from jax.experimental.pallas import tpu as pltpu
from jax.sharding import PartitionSpec as P

HEAD = 64
AXES = ("dp", "tensor")
STEPS = 2


def local_dot(left, right):
    return jnp.dot(left, right, preferred_element_type=jnp.float32)


def dot_rows(left, right):
    return lax.dot_general(
        left, right, (((0,), (0,)), ((), ())), preferred_element_type=jnp.float32
    )


def dot_trans(left, right):
    return lax.dot_general(
        left, right, (((1,), (1,)), ((), ())), preferred_element_type=jnp.float32
    )


def normalize(values):
    centered = values - jnp.mean(values, -1, keepdims=True)
    inverse = lax.rsqrt(jnp.mean(centered * centered, -1, keepdims=True) + 1e-05)
    return (centered * inverse, inverse)


def norm_backward(grad_normed, normed, inverse):
    return inverse * (
        grad_normed
        - jnp.mean(grad_normed, -1, keepdims=True)
        - normed * jnp.mean(grad_normed * normed, -1, keepdims=True)
    )


class Swaps:
    def __init__(self, mesh):
        self.dp = mesh.shape["dp"]
        self.tensor = mesh.shape["tensor"]
        index = lax.axis_index("dp")
        self.masks = [1 << bit for bit in range(self.dp.bit_length() - 1)]
        self.coords = [(index >> bit) & 1 for bit in range(len(self.masks))]
        self.core = lax.axis_index("tensor") % 2

    def move(self, value, target):
        pairs = []
        for row in range(self.dp):
            for column in range(self.tensor):
                to_row, to_column = target(row, column)
                pairs.append((row * self.tensor + column, to_row * self.tensor + to_column))
        return lax.ppermute(value, AXES, pairs)

    def over_core(self, value):
        return self.move(value, lambda row, column: (row, column ^ 1))

    def over_chip(self, value):
        return self.move(value, lambda row, column: (row, column ^ 2))

    def over_dp(self, value, even, odd):
        masks = self.masks
        return self.move(
            value, lambda row, column: (row ^ masks[odd if column % 2 else even], column)
        )

    def plan(self):
        steps = list(range(len(self.masks)))
        result = []
        for even, odd in zip(steps, steps[1::-1] + steps[2:]):
            coord = jnp.where(self.core == 0, self.coords[even], self.coords[odd])
            result.append((even, odd, coord))
        return result


class Order:
    def __init__(self):
        self.last = ()

    def begin(self, *arrays):
        arrays, _ = lax.optimization_barrier((arrays, self.last))
        return arrays[0] if len(arrays) == 1 else arrays

    def end(self, *arrays):
        self.last = arrays
        return arrays[0] if len(arrays) == 1 else arrays


class Total:
    def __init__(self, swaps, order, value, got=None):
        self.swaps, self.order, self.plan = swaps, order, swaps.plan()
        self.queue = [self.first if got is None else self.halve]
        self.queue += [self.halve] * (len(self.plan) - 2)
        self.queue += [self.exchange, self.settle] + [self.double] * (len(self.plan) - 1)
        self.keep, self.got, self.at = value, got, -1
        self.advance()

    def advance(self, count=1):
        for _ in range(count):
            if self.queue:
                self.queue.pop(0)()

    def send(self, value):
        even, odd, _ = self.plan[self.at]
        self.got = self.swaps.over_dp(value, even, odd)

    def first(self):
        self.at = 0
        coord = self.plan[0][2]
        rows = self.keep.shape[0] // 2
        value = self.order.begin(self.keep)
        self.send(self.order.end(pick(value, 1 - coord, rows)))
        self.keep = pick(value, coord, rows)

    def halve(self):
        self.at += 1
        coord = self.plan[self.at][2]
        rows = self.keep.shape[0] // 2
        keep, got = self.order.begin(self.keep, self.got)
        send = pick(keep, 1 - coord, rows) + pick(got, 1 - coord, rows)
        self.keep = pick(keep, coord, rows) + pick(got, coord, rows)
        self.order.end(send, self.keep)
        self.send(send)

    def exchange(self):
        self.at += 1
        keep, got = self.order.begin(self.keep, self.got)
        self.keep = self.order.end(keep + got)
        self.send(self.keep)

    def settle(self):
        keep, got = self.order.begin(self.keep, self.got)
        self.keep = self.order.end(keep + got)
        self.at -= 1
        self.send(self.keep)

    def double(self):
        first = self.plan[self.at][2] == 0
        keep, got = self.order.begin(self.keep, self.got)
        self.keep = self.order.end(
            jnp.concatenate([jnp.where(first, keep, got), jnp.where(first, got, keep)], 0)
        )
        self.at -= 1
        if self.at >= 0:
            self.send(self.keep)

    def finish(self):
        self.advance(len(self.queue))
        return self.keep


VMEM = pl.BlockSpec(memory_space=pltpu.VMEM)


def kernel_call(body, outputs, *arrays, **options):
    shapes = [jax.ShapeDtypeStruct(shape, kind) for shape, kind in outputs]
    options.setdefault("in_specs", [VMEM] * len(arrays))
    options.setdefault("out_specs", [VMEM] * len(shapes))
    return pl.pallas_call(
        body,
        out_shape=shapes,
        cost_estimate=pl.CostEstimate(flops=1, bytes_accessed=1, transcendentals=0),
        compiler_params=pltpu.CompilerParams(vmem_limit_bytes=24 * 1024 * 1024),
        **options,
    )(*arrays)


def join_body(up, up_pair, down, down_pair, up_out, down_out):
    width = up.shape[1]
    up_out[:, :width] = up[...]
    up_out[:, width:] = (up_pair[...] * 0.5).astype(jnp.bfloat16)
    down_out[:width] = down[...]
    down_out[width:] = (down_pair[...] * 0.5).astype(jnp.bfloat16)


def second_body(
    hidden, part, got, cotangent, slope, down, up, bias, gain,
    normed_out, grad_out, low_out, units_out, part_out, sums_out, wide_out,
):
    rows = hidden.shape[0] // 2
    sums = None
    wide = None
    for block in range(2):
        at = pl.ds(block * rows, rows)
        normed, inverse = normalize(hidden[at] + (part[at] + got[at]) + bias[...])
        normed_out[at] = normed
        grad = cotangent[at].astype(jnp.float32)
        terms = [jnp.sum(grad * normed, 0, keepdims=True), jnp.sum(grad, 0, keepdims=True)]
        grad = norm_backward(grad * gain[...], normed, inverse)
        grad_out[at] = grad
        terms.append(jnp.sum(grad, 0, keepdims=True))
        low = grad.astype(jnp.bfloat16)
        low_out[at] = low
        units = (dot_trans(low, down[...]) * slope[at]).astype(jnp.bfloat16)
        units_out[at] = units
        total = jnp.sum(units.astype(jnp.float32), 0, keepdims=True)
        part_out[at] = dot_trans(units, up[...])
        sums = terms if sums is None else [old + new for old, new in zip(sums, terms)]
        wide = total if wide is None else wide + total
    sums_out[...] = jnp.concatenate(sums, 0)
    wide_out[...] = wide


def first_body(
    grad_two, part, got, normed, inverse, gain, own, pair,
    grad_out, low_out, wide_out, own_out, sums_out,
):
    grad = grad_two[...] + (part[...] + got[...])
    terms = [jnp.sum(grad * normed[...], 0, keepdims=True), jnp.sum(grad, 0, keepdims=True)]
    grad = norm_backward(grad * gain[...], normed[...], inverse[...])
    grad_out[...] = grad
    terms.append(jnp.sum(grad, 0, keepdims=True))
    low = grad.astype(jnp.bfloat16)
    low_out[...] = low
    own_out[...] = dot_trans(low, own[...]).astype(jnp.bfloat16)
    wide_out[...] = dot_trans(low, pair[...]).astype(jnp.bfloat16).astype(jnp.float32) * 2.0
    sums_out[...] = jnp.concatenate(terms, 0)


def attention_back_body(query, keys, values, sums, grads, keys_turned, query_out, keys_out, values_out):
    length = query.shape[1]
    rows = min(256, length)
    scale = 1.0 / math.sqrt(HEAD)
    key_rows, value_rows, turned = keys[0], values[0], keys_turned[0]
    key_sum = jnp.zeros((length, HEAD), jnp.float32)
    value_sum = jnp.zeros((length, HEAD), jnp.float32)
    for block in range(length // rows):
        at = pl.ds(block * rows, rows)
        asked, grad = query[0, at], grads[0, at]
        attn = jnp.exp(dot_trans(key_rows, asked) * scale - sums[0, :, at])
        value_sum += local_dot(attn.astype(jnp.bfloat16), grad)
        grad_attn = dot_trans(value_rows, grad)
        mean = jnp.sum(attn * grad_attn, 0, keepdims=True)
        scores = (attn * (grad_attn - mean)).astype(jnp.bfloat16)
        key_sum += local_dot(scores, asked)
        query_out[0, :, at] = (local_dot(turned, scores) * scale).astype(jnp.bfloat16)
    keys_out[0] = (key_sum * scale).astype(jnp.bfloat16)
    values_out[0] = value_sum.astype(jnp.bfloat16)


def pick(block, part, rows):
    return lax.dynamic_slice_in_dim(block, part * rows, rows, 0)


def widen(array):
    return array.astype(jnp.float32) * 2.0


def narrow(array):
    return (array * 0.5).astype(jnp.bfloat16)


def shards(
    mesh,
    frames,
    frame_mask,
    mask_embedding,
    query_weight,
    query_bias,
    key_weight,
    value_weight,
    value_bias,
    out_weight,
    out_bias,
    norm1_gain,
    norm1_shift,
    up_weight,
    up_bias,
    down_weight,
    down_bias,
    norm2_gain,
    norm2_shift,
    cotangent,
):
    swaps = Swaps(mesh)
    order = Order()
    clip_count, length, model_width = frames.shape
    token_rows = clip_count * length
    local_width = query_weight.shape[1]
    heads_here = local_width // HEAD
    score_scale = 1.0 / math.sqrt(HEAD)
    head_shape = (clip_count, length, heads_here, HEAD)
    own_rows = token_rows // 2
    step_rows = own_rows // STEPS
    core = swaps.core
    tensor_index = lax.axis_index("tensor")

    def own_first(array):
        view = array.reshape((2, own_rows) + array.shape[1:])
        return jnp.where(core == 0, view, view[::-1]).reshape(array.shape)

    def step(array, k):
        return array[k * step_rows : (k + 1) * step_rows]

    out_all = lax.all_gather(widen(out_weight), "tensor", tiled=True)
    up_bias_pair = swaps.over_core(up_bias.reshape(1, -1))[0]

    masked_rows = own_first(frame_mask.reshape(token_rows, 1)).astype(jnp.float32)
    masked_in = (
        own_first(frames.reshape(token_rows, model_width)).astype(jnp.float32)
        * (1.0 - masked_rows)
        + masked_rows * mask_embedding
    )
    grad_out = pick(cotangent.reshape(token_rows, model_width), core, own_rows)
    masked_low = masked_in.astype(jnp.bfloat16)
    query = (local_dot(masked_low, query_weight) + query_bias).astype(jnp.bfloat16)
    keys = local_dot(masked_low, key_weight).astype(jnp.bfloat16)
    values = (local_dot(masked_low, value_weight) + value_bias).astype(jnp.bfloat16)
    query_heads = query.reshape(head_shape)
    key_heads = keys.reshape(head_shape)
    value_heads = values.reshape(head_shape)
    scores = (
        jnp.einsum("cqhd,ckhd->chqk", query_heads, key_heads, preferred_element_type=jnp.float32)
        * score_scale
    )
    row_max = jnp.max(scores, -1, keepdims=True)
    expo = jnp.exp(scores - row_max)
    totals = jnp.sum(expo, -1, keepdims=True)
    log_sum = row_max + jnp.log(totals)
    attn_low = (expo / totals).astype(jnp.bfloat16)
    context = jnp.einsum(
        "chqk,ckhd->cqhd", attn_low, value_heads, preferred_element_type=jnp.float32
    )
    context = context.reshape(token_rows, local_width).astype(jnp.bfloat16)

    context_pair = swaps.over_core(widen(context[own_rows:]))
    chip_wide = jnp.concatenate([widen(context[:own_rows]), context_pair], 1)
    other_wide = [swaps.over_chip(step(chip_wide, k)) for k in range(STEPS)]
    order.end(chip_wide)
    up_weight, down_weight = order.begin(up_weight, down_weight)
    up_pair = swaps.over_core(widen(up_weight))
    down_pair = swaps.over_core(widen(down_weight))
    order.end(up_pair, down_pair)
    chip_wide, out_all, up_pair, down_pair = order.begin(chip_wide, out_all, up_pair, down_pair)
    context_chip = narrow(chip_wide)
    out_all = narrow(out_all)
    out_parts = [pick(out_all, tensor_index ^ mask, local_width) for mask in (0, 1, 2, 3)]
    out_chip = jnp.concatenate(out_parts[:2], 0)
    out_other = jnp.concatenate(out_parts[2:], 0)
    units_here = up_weight.shape[1]
    up_chip, down_chip = kernel_call(
        join_body,
        [
            ((model_width, 2 * units_here), jnp.bfloat16),
            ((2 * units_here, model_width), jnp.bfloat16),
        ],
        up_weight,
        up_pair,
        down_weight,
        down_pair,
    )
    up_bias_chip = jnp.concatenate([up_bias, up_bias_pair])
    order.end(context_chip, out_chip, out_other, up_chip, down_chip)

    normed_one, inverse_one, ffn_in, activ, slope = [], [], [], [], []
    hidden_one, ffn_part, ffn_got = [], [], []
    for k in range(STEPS):
        rows, wide = order.begin(step(context_chip, k), other_wide[k])
        attended = local_dot(rows, out_chip) + local_dot(narrow(wide), out_other)
        normed, inverse = normalize(step(masked_in, k) + attended + out_bias)
        hidden = normed * norm1_gain + norm1_shift
        low = hidden.astype(jnp.bfloat16)
        pre_act = local_dot(low, up_chip) + up_bias_chip
        normal_cdf = 0.5 * (1.0 + lax.erf(pre_act / math.sqrt(2.0)))
        normal_pdf = jnp.exp(-0.5 * pre_act * pre_act) / math.sqrt(2.0 * math.pi)
        units = (pre_act * normal_cdf).astype(jnp.bfloat16)
        part = order.end(local_dot(units, down_chip))
        ffn_part.append(part)
        ffn_got.append(swaps.over_chip(part))
        normed_one.append(normed)
        inverse_one.append(inverse)
        hidden_one.append(hidden)
        ffn_in.append(low)
        activ.append(units)
        slope.append(normal_cdf + pre_act * normal_pdf)

    output, grad_h2, grad_h2_low, grad_pre, one_part, one_got = [], [], [], [], [], []
    gain_two, shift_two, bias_down, bias_up = [], [], [], []
    for k in range(STEPS):
        part, got = order.begin(ffn_part[k], ffn_got[k])
        square, wide = (step_rows, model_width), (step_rows, 2 * units_here)
        normed, grad_two, low, units, part, sums, unit_sums = kernel_call(
            second_body,
            [
                (square, jnp.float32),
                (square, jnp.float32),
                (square, jnp.bfloat16),
                (wide, jnp.bfloat16),
                (square, jnp.float32),
                ((3, model_width), jnp.float32),
                ((1, 2 * units_here), jnp.float32),
            ],
            hidden_one[k],
            part,
            got,
            step(grad_out, k),
            slope[k],
            down_chip,
            up_chip,
            down_bias[None],
            norm2_gain[None],
        )
        order.end(part)
        output.append(normed)
        gain_two.append(sums[0])
        shift_two.append(sums[1])
        bias_down.append(sums[2])
        bias_up.append(unit_sums[0])
        one_part.append(part)
        one_got.append(swaps.over_chip(part))
        grad_h2.append(grad_two)
        grad_h2_low.append(low)
        grad_pre.append(units)

    activ = jnp.concatenate(activ, 0)
    grad_h2_low = jnp.concatenate(grad_h2_low, 0)
    activ, grad_h2_low = order.begin(activ, grad_h2_low)
    down_send = order.end(dot_rows(activ[:, units_here:], grad_h2_low))
    down_got = swaps.over_core(down_send)
    activ, grad_h2_low = order.begin(activ, grad_h2_low)
    down_keep = order.end(dot_rows(activ[:, :units_here], grad_h2_low))

    gain_one, shift_one, bias_out, grad_h1, grad_h1_low, wide_context = [], [], [], [], [], []
    context_grads = []
    for k in range(STEPS):
        part, got = order.begin(one_part[k], one_got[k])
        square, narrow_shape = (step_rows, model_width), (step_rows, local_width)
        grad, low, wide, own, sums = kernel_call(
            first_body,
            [
                (square, jnp.float32),
                (square, jnp.bfloat16),
                (narrow_shape, jnp.float32),
                (narrow_shape, jnp.bfloat16),
                ((3, model_width), jnp.float32),
            ],
            grad_h2[k],
            part,
            got,
            normed_one[k],
            inverse_one[k],
            norm1_gain[None],
            out_parts[0],
            out_parts[1],
        )
        gain_one.append(sums[0])
        shift_one.append(sums[1])
        bias_out.append(sums[2])
        grad_h1.append(grad)
        grad_h1_low.append(low)
        wide_context.append(wide)
        context_grads.append(own)
        order.end(wide, own)
        if k == 0:
            ffn_in = jnp.concatenate(ffn_in, 0)
            grad_pre = jnp.concatenate(grad_pre, 0)
            ffn_in, grad_pre = order.begin(ffn_in, grad_pre)
            up_send = order.end(dot_rows(ffn_in, grad_pre[:, units_here:]))
            up_got = swaps.over_core(up_send)
            ffn_in, grad_pre = order.begin(ffn_in, grad_pre)
            up_keep = order.end(dot_rows(ffn_in, grad_pre[:, :units_here]))
            down_total = Total(swaps, order, down_keep, down_got)
            up_total = Total(swaps, order, up_keep, up_got)
    got = swaps.over_core(jnp.concatenate(wide_context, 0))
    grad_context = jnp.concatenate(context_grads + [narrow(got)], 0)
    grad_h1_low = jnp.concatenate(grad_h1_low, 0)

    def by_head(array):
        split = array.reshape(clip_count, length, heads_here, HEAD)
        return split.transpose(0, 2, 1, 3).reshape(clip_count * heads_here, length, HEAD)

    def by_row(array):
        split = array.reshape(clip_count, heads_here, length, HEAD)
        return split.transpose(0, 2, 1, 3).reshape(token_rows, local_width)

    heads = clip_count * heads_here
    head_block = pl.BlockSpec((1, length, HEAD), lambda head: (head, 0, 0))
    turned_block = pl.BlockSpec((1, HEAD, length), lambda head: (head, 0, 0))
    row_block = pl.BlockSpec((1, 1, length), lambda head: (head, 0, 0))
    keys_by_head = by_head(keys)
    operands = (
        by_head(query),
        keys_by_head,
        by_head(values),
        log_sum.reshape(heads, 1, length),
        by_head(grad_context),
        keys_by_head.transpose(0, 2, 1),
    )
    down_total.advance()
    up_total.advance()
    operands = order.begin(*operands)
    grad_query, grad_keys, grad_values = kernel_call(
        attention_back_body,
        [
            ((heads, HEAD, length), jnp.bfloat16),
            ((heads, length, HEAD), jnp.bfloat16),
            ((heads, length, HEAD), jnp.bfloat16),
        ],
        *operands,
        grid=(heads,),
        in_specs=[head_block, head_block, head_block, row_block, head_block, turned_block],
        out_specs=[turned_block, head_block, head_block],
    )
    order.end(grad_query, grad_keys, grad_values)
    down_total.advance()
    grad_query = by_row(grad_query.transpose(0, 2, 1))
    grad_keys = by_row(grad_keys)
    grad_values = by_row(grad_values)
    three = order.end(jnp.concatenate([grad_query, grad_keys, grad_values], 1))
    attn_weight = jnp.concatenate([query_weight, key_weight, value_weight], 1)

    three = order.begin(three)
    terms_send = order.end(dot_trans(three[own_rows:], attn_weight))
    terms_got = swaps.over_core(terms_send)
    three = order.begin(three)
    terms_keep = order.end(dot_trans(three[:own_rows], attn_weight))
    chip_terms, chip_got = [], []
    for k in range(2):
        rows = own_rows // 2
        part, got = order.begin(
            terms_keep[k * rows : (k + 1) * rows], terms_got[k * rows : (k + 1) * rows]
        )
        chip_terms.append(order.end(part + got))
        chip_got.append(swaps.over_chip(chip_terms[-1]))
    grad_h1_low, context_chip = order.begin(grad_h1_low, context_chip)
    out_send = order.end(dot_rows(grad_h1_low, context_chip[:, local_width:]))
    out_got = swaps.over_core(out_send)
    three = order.begin(three)
    three_grad = order.end(dot_rows(masked_low, three))
    out_keep = dot_rows(grad_h1_low, context_chip[:, :local_width])
    out_keep, out_got = order.begin(out_keep, out_got)
    joined = order.end(jnp.concatenate([three_grad, out_keep + out_got], 1))
    attn_total = Total(swaps, order, joined)
    up_total.advance()

    frames_part, mask_sums = [], []
    for k in range(2):
        rows = own_rows // 2
        part, got = order.begin(chip_terms[k], chip_got[k])
        grad_in = jnp.concatenate(grad_h1, 0)[k * rows : (k + 1) * rows] + (part + got)
        mask_sums.append(jnp.sum(grad_in * masked_rows[k * rows : (k + 1) * rows], 0))
        frames_part.append(order.end(grad_in))
        if k == 1:
            up_total.advance()
        down_total.advance()
        attn_total.advance()
    frames_part = jnp.concatenate(frames_part, 0)
    frames_got = swaps.over_core(frames_part)
    output = jnp.concatenate(output, 0)
    output_got = swaps.over_core(output)

    shared = (
        sum(mask_sums),
        sum(bias_out),
        sum(gain_one),
        sum(shift_one),
        sum(bias_down),
        sum(gain_two),
        sum(shift_two),
    )
    own_bias_up = sum(bias_up)
    pair = jnp.concatenate(shared + (own_bias_up[units_here:],))[None]
    mine = jnp.concatenate(shared + (own_bias_up[:units_here],))[None]
    mine, pair_got = order.begin(mine, swaps.over_core(pair))
    packed = mine + pair_got
    packed = jnp.concatenate(
        [
            packed,
            jnp.sum(grad_query.astype(jnp.float32), 0)[None],
            jnp.sum(grad_values.astype(jnp.float32), 0)[None],
        ],
        1,
    )
    order.end(packed)
    for link in range(len(swaps.masks)):
        packed, got = order.begin(packed, swaps.over_dp(packed, link, link))
        packed = order.end(packed + got)
        up_total.advance()
        down_total.advance()
        attn_total.advance()
    pieces = []
    start = 0
    for width in [model_width] * 7 + [units_here] + [local_width] * 2:
        pieces.append(packed[0, start : start + width])
        start += width
    (
        mask_embedding_grad,
        out_bias_grad,
        norm1_gain_grad,
        norm1_shift_grad,
        down_bias_grad,
        norm2_gain_grad,
        norm2_shift_grad,
        up_bias_grad,
        query_bias_grad,
        value_bias_grad,
    ) = pieces
    down_weight_grad = down_total.finish()
    up_weight_grad = up_total.finish()
    attn_weight_grad = attn_total.finish()
    out_weight_grad = attn_weight_grad[:, 3 * local_width :].T
    query_weight_grad = attn_weight_grad[:, :local_width]
    key_weight_grad = attn_weight_grad[:, local_width : 2 * local_width]
    value_weight_grad = attn_weight_grad[:, 2 * local_width : 3 * local_width]

    def in_place(own, got):
        whole = jnp.stack([jnp.where(core == 0, own, got), jnp.where(core == 0, got, own)])
        return whole.reshape(token_rows, model_width)

    frames_grad = in_place(frames_part, frames_got) * (
        1.0 - frame_mask.reshape(token_rows, 1).astype(jnp.float32)
    )
    output = in_place(output, output_got) * norm2_gain + norm2_shift
    return (
        output.astype(jnp.bfloat16).reshape(frames.shape),
        frames_grad.astype(jnp.bfloat16).reshape(frames.shape),
        mask_embedding_grad,
        query_weight_grad,
        query_bias_grad,
        key_weight_grad,
        value_weight_grad,
        value_bias_grad,
        out_weight_grad,
        out_bias_grad,
        norm1_gain_grad,
        norm1_shift_grad,
        up_weight_grad,
        up_bias_grad,
        down_weight_grad,
        down_bias_grad,
        norm2_gain_grad,
        norm2_shift_grad,
    )


def solution(mesh):
    rows, columns, whole, vector = P("dp"), P(None, "tensor"), P(), P("tensor")
    return jax.shard_map(
        lambda *arrays: shards(mesh, *arrays),
        mesh=mesh,
        in_specs=(
            P("dp", None, None),
            P("dp", None),
            whole,
            columns,
            vector,
            columns,
            columns,
            vector,
            P("tensor", None),
            whole,
            whole,
            whole,
            columns,
            vector,
            P("tensor", None),
            whole,
            whole,
            whole,
            P("dp", None, None),
        ),
        out_specs=(
            P("dp", None, None),
            P("dp", None, None),
            whole,
            columns,
            vector,
            columns,
            columns,
            vector,
            P("tensor", None),
            whole,
            whole,
            whole,
            columns,
            vector,
            P("tensor", None),
            whole,
            whole,
            whole,
        ),
        check_vma=False,
    )
```

```python
import math

import jax
import jax.numpy as jnp
from jax import lax
from jax.experimental import pallas as pl
from jax.experimental.pallas import tpu as pltpu
from jax.sharding import PartitionSpec as P

HEAD = 64
AXES = ("dp", "tensor")
STEPS = 2
TURNS = (True, True, True)
ORDER = (
    "Dk", "Ds", "Uk", "N0", "Us", "D1", "U1", "N1", "D2", "U2", "at", "tk", "D3", "ts", "A0",
    "A1", "os", "qk", "T1", "U3", "F0", "D4", "T2", "D5", "F1", "U4", "T3", "V", "V0", "U5",
    "D6", "T4", "V1", "U6", "V2", "T5", "T6",
)


def local_dot(left, right):
    return jnp.dot(left, right, preferred_element_type=jnp.float32)


def dot_rows(left, right):
    return lax.dot_general(
        left, right, (((0,), (0,)), ((), ())), preferred_element_type=jnp.float32
    )


def dot_trans(left, right):
    return lax.dot_general(
        left, right, (((1,), (1,)), ((), ())), preferred_element_type=jnp.float32
    )


def normalize(values):
    centered = values - jnp.mean(values, -1, keepdims=True)
    inverse = lax.rsqrt(jnp.mean(centered * centered, -1, keepdims=True) + 1e-05)
    return (centered * inverse, inverse)


def norm_backward(grad_normed, normed, inverse):
    return inverse * (
        grad_normed
        - jnp.mean(grad_normed, -1, keepdims=True)
        - normed * jnp.mean(grad_normed * normed, -1, keepdims=True)
    )


class Swaps:
    def __init__(self, mesh):
        self.dp = mesh.shape["dp"]
        self.tensor = mesh.shape["tensor"]
        index = lax.axis_index("dp")
        self.masks = [1 << bit for bit in range(self.dp.bit_length() - 1)]
        self.coords = [(index >> bit) & 1 for bit in range(len(self.masks))]
        self.core = lax.axis_index("tensor") % 2

    def move(self, value, target):
        pairs = []
        for row in range(self.dp):
            for column in range(self.tensor):
                to_row, to_column = target(row, column)
                pairs.append((row * self.tensor + column, to_row * self.tensor + to_column))
        return lax.ppermute(value, AXES, pairs)

    def over_core(self, value):
        return self.move(value, lambda row, column: (row, column ^ 1))

    def over_chip(self, value):
        return self.move(value, lambda row, column: (row, column ^ 2))

    def over_dp(self, value, even, odd):
        masks = self.masks
        return self.move(
            value, lambda row, column: (row ^ masks[odd if column % 2 else even], column)
        )

    def plan(self, turn):
        steps = list(range(len(self.masks)))
        turned = steps[1::-1] + steps[2:] if turn else steps
        result = []
        for even, odd in zip(steps, turned):
            coord = jnp.where(self.core == 0, self.coords[even], self.coords[odd])
            result.append((even, odd, coord))
        return result


class Order:
    def __init__(self):
        self.last = ()

    def begin(self, *arrays):
        arrays, _ = lax.optimization_barrier((arrays, self.last))
        self.last = ()
        return arrays[0] if len(arrays) == 1 else arrays

    def end(self, *arrays):
        self.last += arrays
        return arrays[0] if len(arrays) == 1 else arrays


class Total:
    def __init__(self, swaps, order, turn):
        self.swaps, self.order, self.plan = swaps, order, swaps.plan(turn)
        self.queue = [self.first] + [self.halve] * (len(self.plan) - 2)
        self.queue += [self.exchange, self.settle] + [self.double] * (len(self.plan) - 1)

    def load(self, value, got=None):
        self.keep, self.got, self.at = value, got, -1
        self.queue.pop(0) if got is None else None
        if got is None:
            self.first()
        else:
            self.queue[0] = self.halve
            self.advance()

    def advance(self, count=1):
        for _ in range(count):
            if self.queue:
                self.queue.pop(0)()

    def send(self, value):
        even, odd, _ = self.plan[self.at]
        self.got = self.swaps.over_dp(value, even, odd)

    def first(self):
        self.at = 0
        coord = self.plan[0][2]
        rows = self.keep.shape[0] // 2
        value = self.order.begin(self.keep)
        self.send(self.order.end(pick(value, 1 - coord, rows)))
        self.keep = pick(value, coord, rows)

    def halve(self):
        self.at += 1
        coord = self.plan[self.at][2]
        rows = self.keep.shape[0] // 2
        keep, got = self.order.begin(self.keep, self.got)
        send = pick(keep, 1 - coord, rows) + pick(got, 1 - coord, rows)
        self.keep = pick(keep, coord, rows) + pick(got, coord, rows)
        self.order.end(send, self.keep)
        self.send(send)

    def exchange(self):
        self.at += 1
        keep, got = self.order.begin(self.keep, self.got)
        self.keep = self.order.end(keep + got)
        self.send(self.keep)

    def settle(self):
        keep, got = self.order.begin(self.keep, self.got)
        self.keep = self.order.end(keep + got)
        self.at -= 1
        self.send(self.keep)

    def double(self):
        first = self.plan[self.at][2] == 0
        keep, got = self.order.begin(self.keep, self.got)
        self.keep = self.order.end(
            jnp.concatenate([jnp.where(first, keep, got), jnp.where(first, got, keep)], 0)
        )
        self.at -= 1
        if self.at >= 0:
            self.send(self.keep)

    def finish(self):
        self.advance(len(self.queue))
        return self.keep


VMEM = pl.BlockSpec(memory_space=pltpu.VMEM)
SMEM = pl.BlockSpec(memory_space=pltpu.SMEM)


def kernel_call(body, outputs, *arrays, **options):
    shapes = [jax.ShapeDtypeStruct(shape, kind) for shape, kind in outputs]
    options.setdefault("in_specs", [VMEM] * len(arrays))
    options.setdefault("out_specs", [VMEM] * len(shapes))
    return pl.pallas_call(
        body,
        out_shape=shapes,
        cost_estimate=pl.CostEstimate(flops=1, bytes_accessed=1, transcendentals=0),
        compiler_params=pltpu.CompilerParams(vmem_limit_bytes=24 * 1024 * 1024),
        **options,
    )(*arrays)


def send_body(context, send_out, own_out):
    rows = send_out.shape[0]
    send_out[...] = context[rows:].astype(jnp.float32) * 2.0
    own_out[...] = context[:rows].astype(jnp.float32) * 2.0


def pack_body(own, pair, *outs):
    *steps, chip_out = outs
    rows, width = steps[0].shape[0], own.shape[1]
    for index, out in enumerate(steps):
        at = slice(index * rows, (index + 1) * rows)
        out[:, :width] = own[at]
        out[:, width:] = pair[at]
        chip_out[at, :width] = (own[at] * 0.5).astype(jnp.bfloat16)
        chip_out[at, width:] = (pair[at] * 0.5).astype(jnp.bfloat16)


def join_body(
    index, up, up_pair, down, down_pair, bias, bias_pair, out_all,
    up_out, down_out, bias_out, chip_out, other_out,
):
    width = up.shape[1]
    up_out[:, :width] = up[...]
    up_out[:, width:] = (up_pair[...] * 0.5).astype(jnp.bfloat16)
    down_out[:width] = down[...]
    down_out[width:] = (down_pair[...] * 0.5).astype(jnp.bfloat16)
    bias_out[:, :width] = bias[...]
    bias_out[:, width:] = bias_pair[...]
    rows = chip_out.shape[0] // 2
    for mask, out in enumerate((chip_out, chip_out, other_out, other_out)):
        at = pl.ds(pl.multiple_of((index[0] ^ mask) * rows, 8), rows)
        to = slice(mask % 2 * rows, (mask % 2 + 1) * rows)
        out[to] = (out_all[at] * 0.5).astype(jnp.bfloat16)


def second_body(
    hidden, part, got, cotangent, slope, down, up, bias, gain,
    normed_out, grad_out, low_out, units_out, part_out, sums_out, wide_out,
):
    rows = hidden.shape[0] // 2
    sums_out[...] = jnp.zeros_like(sums_out)
    wide_out[...] = jnp.zeros_like(wide_out)

    def one(block, carry):
        at = pl.ds(pl.multiple_of(block * rows, 8), rows)
        normed, inverse = normalize(hidden[at] + (part[at] + got[at]) + bias[...])
        normed_out[at] = normed
        grad = cotangent[at].astype(jnp.float32)
        sums_out[0:1] += jnp.sum(grad * normed, 0, keepdims=True)
        sums_out[1:2] += jnp.sum(grad, 0, keepdims=True)
        grad = norm_backward(grad * gain[...], normed, inverse)
        grad_out[at] = grad
        sums_out[2:3] += jnp.sum(grad, 0, keepdims=True)
        low = grad.astype(jnp.bfloat16)
        low_out[at] = low
        units = (dot_trans(low, down[...]) * slope[at]).astype(jnp.bfloat16)
        units_out[at] = units
        wide_out[...] += jnp.sum(units.astype(jnp.float32), 0, keepdims=True)
        part_out[at] = dot_trans(units, up[...])
        return carry

    lax.fori_loop(0, 2, one, 0)


def first_body(
    grad_two, part, got, normed, inverse, gain, own, pair,
    grad_out, low_out, wide_out, own_out, sums_out,
):
    rows = part.shape[0] // 2
    sums_out[...] = jnp.zeros_like(sums_out)

    def one(block, carry):
        at = pl.ds(pl.multiple_of(block * rows, 8), rows)
        grad = grad_two[at] + (part[at] + got[at])
        sums_out[0:1] += jnp.sum(grad * normed[at], 0, keepdims=True)
        sums_out[1:2] += jnp.sum(grad, 0, keepdims=True)
        grad = norm_backward(grad * gain[...], normed[at], inverse[at])
        grad_out[at] = grad
        sums_out[2:3] += jnp.sum(grad, 0, keepdims=True)
        low = grad.astype(jnp.bfloat16)
        low_out[at] = low
        own_out[at] = dot_trans(low, own[...]).astype(jnp.bfloat16)
        turned = dot_trans(low, pair[...]).astype(jnp.bfloat16)
        wide_out[at] = turned.astype(jnp.float32) * 2.0
        return carry

    lax.fori_loop(0, 2, one, 0)


def attention_back_body(query, keys, values, sums, grads, keys_turned, query_out, keys_out, values_out):
    length = query.shape[1]
    rows = min(256, length)
    scale = 1.0 / math.sqrt(HEAD)
    key_rows, value_rows, turned = keys[0], values[0], keys_turned[0]
    key_sum = jnp.zeros((length, HEAD), jnp.float32)
    value_sum = jnp.zeros((length, HEAD), jnp.float32)
    for block in range(length // rows):
        at = pl.ds(block * rows, rows)
        asked, grad = query[0, at], grads[0, at]
        attn = jnp.exp(dot_trans(key_rows, asked) * scale - sums[0, :, at])
        value_sum += local_dot(attn.astype(jnp.bfloat16), grad)
        grad_attn = dot_trans(value_rows, grad)
        mean = jnp.sum(attn * grad_attn, 0, keepdims=True)
        scores = (attn * (grad_attn - mean)).astype(jnp.bfloat16)
        key_sum += local_dot(scores, asked)
        query_out[0, :, at] = (local_dot(turned, scores) * scale).astype(jnp.bfloat16)
    keys_out[0] = (key_sum * scale).astype(jnp.bfloat16)
    values_out[0] = value_sum.astype(jnp.bfloat16)


def pick(block, part, rows):
    return lax.dynamic_slice_in_dim(block, part * rows, rows, 0)


def widen(array):
    return array.astype(jnp.float32) * 2.0


def narrow(array):
    return (array * 0.5).astype(jnp.bfloat16)


def shards(
    mesh,
    frames,
    frame_mask,
    mask_embedding,
    query_weight,
    query_bias,
    key_weight,
    value_weight,
    value_bias,
    out_weight,
    out_bias,
    norm1_gain,
    norm1_shift,
    up_weight,
    up_bias,
    down_weight,
    down_bias,
    norm2_gain,
    norm2_shift,
    cotangent,
):
    swaps = Swaps(mesh)
    order = Order()
    clip_count, length, model_width = frames.shape
    token_rows = clip_count * length
    local_width = query_weight.shape[1]
    heads_here = local_width // HEAD
    score_scale = 1.0 / math.sqrt(HEAD)
    head_shape = (clip_count, length, heads_here, HEAD)
    own_rows = token_rows // 2
    step_rows = own_rows // STEPS
    core = swaps.core
    tensor_index = lax.axis_index("tensor")

    def step(array, k):
        return array[k * step_rows : (k + 1) * step_rows]

    out_all = lax.all_gather(widen(out_weight), "tensor", tiled=True)
    up_wide, down_wide = widen(up_weight), widen(down_weight)
    up_pair = swaps.over_core(up_wide)
    down_pair = swaps.over_core(down_wide)
    order.end(up_wide, down_wide)
    up_bias_row = up_bias.reshape(1, -1)
    up_bias_pair = swaps.over_core(up_bias_row)

    def masked(part):
        rows = pick(frame_mask.reshape(token_rows, 1), part, own_rows).astype(jnp.float32)
        block = pick(frames.reshape(token_rows, model_width), part, own_rows)
        return block.astype(jnp.float32) * (1.0 - rows) + rows * mask_embedding, rows

    masked_in, masked_rows = masked(core)
    masked_low = jnp.concatenate(
        [masked_in.astype(jnp.bfloat16), masked(1 - core)[0].astype(jnp.bfloat16)], 0
    )
    grad_out = pick(cotangent.reshape(token_rows, model_width), core, own_rows)
    masked_low = order.begin(masked_low)
    query = (local_dot(masked_low, query_weight) + query_bias).astype(jnp.bfloat16)
    keys = local_dot(masked_low, key_weight).astype(jnp.bfloat16)
    values = (local_dot(masked_low, value_weight) + value_bias).astype(jnp.bfloat16)
    query_heads = query.reshape(head_shape)
    key_heads = keys.reshape(head_shape)
    value_heads = values.reshape(head_shape)
    scores = (
        jnp.einsum("cqhd,ckhd->chqk", query_heads, key_heads, preferred_element_type=jnp.float32)
        * score_scale
    )
    row_max = jnp.max(scores, -1, keepdims=True)
    expo = jnp.exp(scores - row_max)
    totals = jnp.sum(expo, -1, keepdims=True)
    log_sum = row_max + jnp.log(totals)
    attn_low = (expo / totals).astype(jnp.bfloat16)
    context = jnp.einsum(
        "chqk,ckhd->cqhd", attn_low, value_heads, preferred_element_type=jnp.float32
    )
    context = context.reshape(token_rows, local_width).astype(jnp.bfloat16)

    narrow_half = (own_rows, local_width)
    context_send, context_own = kernel_call(
        send_body, [(narrow_half, jnp.float32)] * 2, order.begin(context)
    )
    order.end(context_send)
    context_pair = swaps.over_core(context_send)
    chip_step = (step_rows, 2 * local_width)
    *chip_steps, context_chip = kernel_call(
        pack_body,
        [(chip_step, jnp.float32)] * STEPS + [((own_rows, chip_step[1]), jnp.bfloat16)],
        *order.begin(context_own, context_pair),
    )
    order.end(*chip_steps, context_chip)
    other_wide = [swaps.over_chip(block) for block in chip_steps]
    out_all, up_pair, down_pair = order.begin(out_all, up_pair, down_pair)
    units_here = up_weight.shape[1]
    operands = (
        tensor_index.reshape(1),
        up_weight,
        up_pair,
        down_weight,
        down_pair,
        up_bias_row,
        up_bias_pair,
        out_all,
    )
    up_chip, down_chip, up_bias_chip, out_chip, out_other = kernel_call(
        join_body,
        [
            ((model_width, 2 * units_here), jnp.bfloat16),
            ((2 * units_here, model_width), jnp.bfloat16),
            ((1, 2 * units_here), jnp.float32),
            ((2 * local_width, model_width), jnp.bfloat16),
            ((2 * local_width, model_width), jnp.bfloat16),
        ],
        *operands,
        in_specs=[SMEM] + [VMEM] * 7,
    )
    out_parts = [out_chip[:local_width], out_chip[local_width:]]
    order.end(out_chip, out_other, up_chip, down_chip)

    normed_one, inverse_one, ffn_in, activ, slope = [], [], [], [], []
    hidden_one, ffn_part, ffn_got = [], [], []
    for k in range(STEPS):
        rows, wide = order.begin(step(context_chip, k), other_wide[k])
        attended = local_dot(rows, out_chip) + local_dot(narrow(wide), out_other)
        normed, inverse = normalize(step(masked_in, k) + attended + out_bias)
        hidden = normed * norm1_gain + norm1_shift
        low = hidden.astype(jnp.bfloat16)
        pre_act = local_dot(low, up_chip) + up_bias_chip
        normal_cdf = 0.5 * (1.0 + lax.erf(pre_act / math.sqrt(2.0)))
        normal_pdf = jnp.exp(-0.5 * pre_act * pre_act) / math.sqrt(2.0 * math.pi)
        units = (pre_act * normal_cdf).astype(jnp.bfloat16)
        part = order.end(local_dot(units, down_chip))
        ffn_part.append(part)
        ffn_got.append(swaps.over_chip(part))
        normed_one.append(normed)
        inverse_one.append(inverse)
        hidden_one.append(hidden)
        ffn_in.append(low)
        activ.append(units)
        slope.append(normal_cdf + pre_act * normal_pdf)

    def by_head(array):
        split = array.reshape(clip_count, length, heads_here, HEAD)
        return split.transpose(0, 2, 1, 3).reshape(clip_count * heads_here, length, HEAD)

    query, keys, values = order.begin(query, keys, values)
    keys_by_head = by_head(keys)
    attention_operands = order.end(
        by_head(query),
        keys_by_head,
        by_head(values),
        log_sum.reshape(clip_count * heads_here, 1, length),
        keys_by_head.transpose(0, 2, 1),
    )
    output, grad_h2, grad_h2_low, grad_pre, one_part, one_got = [], [], [], [], [], []
    gain_two, shift_two, bias_down, bias_up = [], [], [], []
    for k in range(STEPS):
        part, got = order.begin(ffn_part[k], ffn_got[k])
        square, wide = (step_rows, model_width), (step_rows, 2 * units_here)
        normed, grad_two, low, units, part, sums, unit_sums = kernel_call(
            second_body,
            [
                (square, jnp.float32),
                (square, jnp.float32),
                (square, jnp.bfloat16),
                (wide, jnp.bfloat16),
                (square, jnp.float32),
                ((3, model_width), jnp.float32),
                ((1, 2 * units_here), jnp.float32),
            ],
            hidden_one[k],
            part,
            got,
            step(grad_out, k),
            slope[k],
            down_chip,
            up_chip,
            down_bias[None],
            norm2_gain[None],
        )
        order.end(part)
        output.append(normed)
        gain_two.append(sums[0])
        shift_two.append(sums[1])
        bias_down.append(sums[2])
        bias_up.append(unit_sums[0])
        one_part.append(part)
        one_got.append(swaps.over_chip(part))
        grad_h2.append(grad_two)
        grad_h2_low.append(low)
        grad_pre.append(units)

    activ = jnp.concatenate(activ, 0)
    ffn_in = jnp.concatenate(ffn_in, 0)
    grad_h2_low = jnp.concatenate(grad_h2_low, 0)
    grad_pre = jnp.concatenate(grad_pre, 0)
    totals = {name: Total(swaps, order, turn) for name, turn in zip("DUT", TURNS)}
    v = {}
    heads = clip_count * heads_here
    rows = own_rows // 2

    def by_row(array):
        split = array.reshape(clip_count, heads_here, length, HEAD)
        return split.transpose(0, 2, 1, 3).reshape(token_rows, local_width)

    def weight_grad(left, right):
        return order.end(dot_rows(*order.begin(left, right)))

    def down_send():
        send = weight_grad(activ[:, units_here:], grad_h2_low)
        v["down_got"] = swaps.over_core(send)

    def down_keep():
        v["down"] = weight_grad(activ[:, :units_here], grad_h2_low)

    def up_send():
        send = weight_grad(ffn_in, grad_pre[:, units_here:])
        v["up_got"] = swaps.over_core(send)

    def up_keep():
        v["up"] = weight_grad(ffn_in, grad_pre[:, :units_here])

    def first_norm(k):
        part, got = order.begin(one_part[k], one_got[k])
        square, narrow_shape = (step_rows, model_width), (step_rows, local_width)
        v["one", k] = kernel_call(
            first_body,
            [
                (square, jnp.float32),
                (square, jnp.bfloat16),
                (narrow_shape, jnp.float32),
                (narrow_shape, jnp.bfloat16),
                ((3, model_width), jnp.float32),
            ],
            grad_h2[k],
            part,
            got,
            normed_one[k],
            inverse_one[k],
            norm1_gain[None],
            out_parts[0],
            out_parts[1],
        )
        order.end(v["one", k][2], v["one", k][3])
        if k == STEPS - 1:
            kernels = [v["one", at] for at in range(STEPS)]
            v["context_got"] = swaps.over_core(jnp.concatenate([one[2] for one in kernels], 0))
            v["context_own"] = [one[3] for one in kernels]
            v["h1_low"] = jnp.concatenate([one[1] for one in kernels], 0)
            v["h1"] = jnp.concatenate([one[0] for one in kernels], 0)

    def attention():
        grad_context = jnp.concatenate(v["context_own"] + [narrow(v["context_got"])], 0)
        head_block = pl.BlockSpec((1, length, HEAD), lambda head: (head, 0, 0))
        turned_block = pl.BlockSpec((1, HEAD, length), lambda head: (head, 0, 0))
        row_block = pl.BlockSpec((1, 1, length), lambda head: (head, 0, 0))
        operands = attention_operands[:4] + (by_head(grad_context),) + attention_operands[4:]
        grad_query, grad_keys, grad_values = kernel_call(
            attention_back_body,
            [
                ((heads, HEAD, length), jnp.bfloat16),
                ((heads, length, HEAD), jnp.bfloat16),
                ((heads, length, HEAD), jnp.bfloat16),
            ],
            *order.begin(*operands),
            grid=(heads,),
            in_specs=[head_block, head_block, head_block, row_block, head_block, turned_block],
            out_specs=[turned_block, head_block, head_block],
        )
        order.end(grad_query, grad_keys, grad_values)
        v["query"] = by_row(grad_query.transpose(0, 2, 1))
        v["values"] = by_row(grad_values)
        v["three"] = jnp.concatenate([v["query"], by_row(grad_keys), v["values"]], 1)

    attn_weight = jnp.concatenate([query_weight, key_weight, value_weight], 1)

    def terms_send():
        v["three"] = order.begin(v["three"])
        send = order.end(dot_trans(v["three"][own_rows:], attn_weight))
        v["terms_got"] = swaps.over_core(send)

    def terms_keep():
        three = order.begin(v["three"])
        v["terms"] = order.end(dot_trans(three[:own_rows], attn_weight))

    def chip_terms(k):
        at = slice(k * rows, (k + 1) * rows)
        part, got = order.begin(v["terms"][at], v["terms_got"][at])
        v["chip", k] = order.end(part + got)
        v["chip_got", k] = swaps.over_chip(v["chip", k])

    def out_send():
        send = weight_grad(v["h1_low"], context_chip[:, local_width:])
        v["out_got"] = swaps.over_core(send)

    def three_grad():
        v["three_grad"] = weight_grad(masked_low, v["three"])

    def join():
        keep, got = order.begin(
            dot_rows(v["h1_low"], context_chip[:, :local_width]), v["out_got"]
        )
        joined = order.end(jnp.concatenate([v["three_grad"], keep + got], 1))
        totals["T"].load(joined)

    def frames_step(k):
        at = slice(k * rows, (k + 1) * rows)
        part, got = order.begin(v["chip", k], v["chip_got", k])
        grad_in = v["h1"][at] + (part + got)
        v["mask", k] = jnp.sum(grad_in * masked_rows[at], 0)
        v["frames", k] = order.end(grad_in)

    def vectors():
        kernels = [v["one", at][4] for at in range(STEPS)]
        shared = (
            v["mask", 0] + v["mask", 1],
            sum(sums[2] for sums in kernels),
            sum(sums[0] for sums in kernels),
            sum(sums[1] for sums in kernels),
            sum(bias_down),
            sum(gain_two),
            sum(shift_two),
        )
        own_bias_up = sum(bias_up)
        pair = jnp.concatenate(shared + (own_bias_up[units_here:],))[None]
        mine = jnp.concatenate(shared + (own_bias_up[:units_here],))[None]
        mine, pair_got = order.begin(mine, swaps.over_core(pair))
        attention_bias = [
            jnp.sum(v[name].astype(jnp.float32), 0)[None] for name in ("query", "values")
        ]
        v["packed"] = order.end(jnp.concatenate([mine + pair_got] + attention_bias, 1))

    def vector_step(link):
        packed, got = order.begin(v["packed"], swaps.over_dp(v["packed"], link, link))
        v["packed"] = order.end(packed + got)

    stages = {
        "Ds": down_send,
        "Dk": down_keep,
        "Us": up_send,
        "Uk": up_keep,
        "N0": lambda: first_norm(0),
        "N1": lambda: first_norm(1),
        "at": attention,
        "ts": terms_send,
        "tk": terms_keep,
        "A0": lambda: chip_terms(0),
        "A1": lambda: chip_terms(1),
        "os": out_send,
        "qk": three_grad,
        "T1": join,
        "F0": lambda: frames_step(0),
        "F1": lambda: frames_step(1),
        "V": vectors,
        "V0": lambda: vector_step(0),
        "V1": lambda: vector_step(1),
        "V2": lambda: [vector_step(link) for link in range(2, len(swaps.masks))],
        "D1": lambda: totals["D"].load(v["down"], v["down_got"]),
        "U1": lambda: totals["U"].load(v["up"], v["up_got"]),
    }
    for name in ORDER:
        stages[name]() if name in stages else totals[name[0]].advance()
    frames_part = jnp.concatenate([v["frames", 0], v["frames", 1]], 0)
    frames_got = swaps.over_core(frames_part)
    output = jnp.concatenate(output, 0)
    output_got = swaps.over_core(output)
    packed = v["packed"]
    pieces = []
    start = 0
    for width in [model_width] * 7 + [units_here] + [local_width] * 2:
        pieces.append(packed[0, start : start + width])
        start += width
    (
        mask_embedding_grad,
        out_bias_grad,
        norm1_gain_grad,
        norm1_shift_grad,
        down_bias_grad,
        norm2_gain_grad,
        norm2_shift_grad,
        up_bias_grad,
        query_bias_grad,
        value_bias_grad,
    ) = pieces
    down_weight_grad, up_weight_grad, attn_weight_grad = (totals[name].finish() for name in "DUT")
    out_weight_grad = attn_weight_grad[:, 3 * local_width :].T
    query_weight_grad = attn_weight_grad[:, :local_width]
    key_weight_grad = attn_weight_grad[:, local_width : 2 * local_width]
    value_weight_grad = attn_weight_grad[:, 2 * local_width : 3 * local_width]

    def in_place(own, got):
        whole = jnp.stack([jnp.where(core == 0, own, got), jnp.where(core == 0, got, own)])
        return whole.reshape(token_rows, model_width)

    frames_grad = in_place(frames_part, frames_got) * (
        1.0 - frame_mask.reshape(token_rows, 1).astype(jnp.float32)
    )
    output = in_place(output, output_got) * norm2_gain + norm2_shift
    return (
        output.astype(jnp.bfloat16).reshape(frames.shape),
        frames_grad.astype(jnp.bfloat16).reshape(frames.shape),
        mask_embedding_grad,
        query_weight_grad,
        query_bias_grad,
        key_weight_grad,
        value_weight_grad,
        value_bias_grad,
        out_weight_grad,
        out_bias_grad,
        norm1_gain_grad,
        norm1_shift_grad,
        up_weight_grad,
        up_bias_grad,
        down_weight_grad,
        down_bias_grad,
        norm2_gain_grad,
        norm2_shift_grad,
    )


def solution(mesh):
    rows, columns, whole, vector = P("dp"), P(None, "tensor"), P(), P("tensor")
    return jax.shard_map(
        lambda *arrays: shards(mesh, *arrays),
        mesh=mesh,
        in_specs=(
            P("dp", None, None),
            P("dp", None),
            whole,
            columns,
            vector,
            columns,
            columns,
            vector,
            P("tensor", None),
            whole,
            whole,
            whole,
            columns,
            vector,
            P("tensor", None),
            whole,
            whole,
            whole,
            P("dp", None, None),
        ),
        out_specs=(
            P("dp", None, None),
            P("dp", None, None),
            whole,
            columns,
            vector,
            columns,
            columns,
            vector,
            P("tensor", None),
            whole,
            whole,
            whole,
            columns,
            vector,
            P("tensor", None),
            whole,
            whole,
            whole,
        ),
        check_vma=False,
    )
```

```python
import math

import jax
import jax.numpy as jnp
from jax import lax
from jax.experimental import pallas as pl
from jax.experimental.pallas import tpu as pltpu
from jax.sharding import PartitionSpec as P

HEAD = 64
AXES = ("dp", "tensor")
STEPS = 2
TURNS = (True, True, True)
ORDER = (
    "Dk", "Ds", "Uk", "N0", "Us", "D1", "U1", "N1", "D2", "U2", "at", "tk", "D3", "ts", "A0",
    "A1", "os", "qk", "T1", "U3", "F0", "D4", "T2", "D5", "F1", "U4", "T3", "V", "U5", "T4",
    "V0", "D6", "V1", "T5", "U6", "V2", "T6",
)


def local_dot(left, right):
    return jnp.dot(left, right, preferred_element_type=jnp.float32)


def dot_rows(left, right):
    return lax.dot_general(
        left, right, (((0,), (0,)), ((), ())), preferred_element_type=jnp.float32
    )


def dot_trans(left, right):
    return lax.dot_general(
        left, right, (((1,), (1,)), ((), ())), preferred_element_type=jnp.float32
    )


def normalize(values):
    centered = values - jnp.mean(values, -1, keepdims=True)
    inverse = lax.rsqrt(jnp.mean(centered * centered, -1, keepdims=True) + 1e-05)
    return (centered * inverse, inverse)


def norm_backward(grad_normed, normed, inverse):
    return inverse * (
        grad_normed
        - jnp.mean(grad_normed, -1, keepdims=True)
        - normed * jnp.mean(grad_normed * normed, -1, keepdims=True)
    )


class Swaps:
    def __init__(self, mesh):
        self.dp = mesh.shape["dp"]
        self.tensor = mesh.shape["tensor"]
        index = lax.axis_index("dp")
        self.masks = [1 << bit for bit in range(self.dp.bit_length() - 1)]
        self.coords = [(index >> bit) & 1 for bit in range(len(self.masks))]
        self.core = lax.axis_index("tensor") % 2

    def move(self, value, target):
        pairs = []
        for row in range(self.dp):
            for column in range(self.tensor):
                to_row, to_column = target(row, column)
                pairs.append((row * self.tensor + column, to_row * self.tensor + to_column))
        return lax.ppermute(value, AXES, pairs)

    def over_core(self, value):
        return self.move(value, lambda row, column: (row, column ^ 1))

    def over_chip(self, value):
        return self.move(value, lambda row, column: (row, column ^ 2))

    def over_dp(self, value, even, odd):
        masks = self.masks
        return self.move(
            value, lambda row, column: (row ^ masks[odd if column % 2 else even], column)
        )

    def plan(self, turn):
        steps = list(range(len(self.masks)))
        turned = steps[1::-1] + steps[2:] if turn else steps
        result = []
        for even, odd in zip(steps, turned):
            coord = jnp.where(self.core == 0, self.coords[even], self.coords[odd])
            result.append((even, odd, coord))
        return result


class Order:
    def __init__(self):
        self.last = ()

    def begin(self, *arrays):
        arrays, _ = lax.optimization_barrier((arrays, self.last))
        self.last = ()
        return arrays[0] if len(arrays) == 1 else arrays

    def end(self, *arrays):
        self.last += arrays
        return arrays[0] if len(arrays) == 1 else arrays


class Total:
    def __init__(self, swaps, order, turn):
        self.swaps, self.order, self.plan = swaps, order, swaps.plan(turn)
        self.queue = [self.first] + [self.halve] * (len(self.plan) - 2)
        self.queue += [self.exchange, self.settle] + [self.double] * (len(self.plan) - 1)

    def load(self, value, got=None):
        self.keep, self.got, self.at = value, got, -1
        self.queue.pop(0) if got is None else None
        if got is None:
            self.first()
        else:
            self.queue[0] = self.halve
            self.advance()

    def advance(self, count=1):
        for _ in range(count):
            if self.queue:
                self.queue.pop(0)()

    def send(self, value):
        even, odd, _ = self.plan[self.at]
        self.got = self.swaps.over_dp(value, even, odd)

    def first(self):
        self.at = 0
        coord = self.plan[0][2]
        rows = self.keep.shape[0] // 2
        value = self.order.begin(self.keep)
        self.send(self.order.end(pick(value, 1 - coord, rows)))
        self.keep = pick(value, coord, rows)

    def halve(self):
        self.at += 1
        coord = self.plan[self.at][2]
        rows = self.keep.shape[0] // 2
        keep, got = self.order.begin(self.keep, self.got)
        send = pick(keep, 1 - coord, rows) + pick(got, 1 - coord, rows)
        self.keep = pick(keep, coord, rows) + pick(got, coord, rows)
        self.order.end(send, self.keep)
        self.send(send)

    def exchange(self):
        self.at += 1
        keep, got = self.order.begin(self.keep, self.got)
        self.keep = self.order.end(keep + got)
        self.send(self.keep)

    def settle(self):
        keep, got = self.order.begin(self.keep, self.got)
        self.keep = self.order.end(keep + got)
        self.at -= 1
        self.send(self.keep)

    def double(self):
        first = self.plan[self.at][2] == 0
        keep, got = self.order.begin(self.keep, self.got)
        self.keep = self.order.end(
            jnp.concatenate([jnp.where(first, keep, got), jnp.where(first, got, keep)], 0)
        )
        self.at -= 1
        if self.at >= 0:
            self.send(self.keep)

    def finish(self):
        self.advance(len(self.queue))
        return self.keep


VMEM = pl.BlockSpec(memory_space=pltpu.VMEM)
SMEM = pl.BlockSpec(memory_space=pltpu.SMEM)


def kernel_call(body, outputs, *arrays, **options):
    shapes = [jax.ShapeDtypeStruct(shape, kind) for shape, kind in outputs]
    options.setdefault("in_specs", [VMEM] * len(arrays))
    options.setdefault("out_specs", [VMEM] * len(shapes))
    return pl.pallas_call(
        body,
        out_shape=shapes,
        cost_estimate=pl.CostEstimate(flops=1, bytes_accessed=1, transcendentals=0),
        compiler_params=pltpu.CompilerParams(vmem_limit_bytes=24 * 1024 * 1024),
        **options,
    )(*arrays)


def send_body(context, send_out, own_out):
    rows = send_out.shape[0]
    send_out[...] = context[rows:].astype(jnp.float32) * 2.0
    own_out[...] = context[:rows].astype(jnp.float32) * 2.0


def pack_body(own, pair, *outs):
    *steps, chip_out = outs
    rows, width = steps[0].shape[0], own.shape[1]
    for index, out in enumerate(steps):
        at = slice(index * rows, (index + 1) * rows)
        out[:, :width] = own[at]
        out[:, width:] = pair[at]
        chip_out[at, :width] = (own[at] * 0.5).astype(jnp.bfloat16)
        chip_out[at, width:] = (pair[at] * 0.5).astype(jnp.bfloat16)


def join_body(
    index, up, up_pair, down, down_pair, bias, bias_pair, out_all,
    up_out, down_out, bias_out, chip_out, other_out,
):
    width = up.shape[1]
    up_out[:, :width] = up[...]
    up_out[:, width:] = (up_pair[...] * 0.5).astype(jnp.bfloat16)
    down_out[:width] = down[...]
    down_out[width:] = (down_pair[...] * 0.5).astype(jnp.bfloat16)
    bias_out[:, :width] = bias[...]
    bias_out[:, width:] = bias_pair[...]
    rows = chip_out.shape[0] // 2
    for mask, out in enumerate((chip_out, chip_out, other_out, other_out)):
        at = pl.ds(pl.multiple_of((index[0] ^ mask) * rows, 8), rows)
        to = slice(mask % 2 * rows, (mask % 2 + 1) * rows)
        out[to] = (out_all[at] * 0.5).astype(jnp.bfloat16)


def second_body(
    hidden, part, got, cotangent, slope, down, up, bias, gain,
    normed_out, grad_out, low_out, units_out, part_out, sums_out, wide_out,
):
    rows = hidden.shape[0] // 2
    sums_out[...] = jnp.zeros_like(sums_out)
    wide_out[...] = jnp.zeros_like(wide_out)

    def one(block, carry):
        at = pl.ds(pl.multiple_of(block * rows, 8), rows)
        normed, inverse = normalize(hidden[at] + (part[at] + got[at]) + bias[...])
        normed_out[at] = normed
        grad = cotangent[at].astype(jnp.float32)
        sums_out[0:1] += jnp.sum(grad * normed, 0, keepdims=True)
        sums_out[1:2] += jnp.sum(grad, 0, keepdims=True)
        grad = norm_backward(grad * gain[...], normed, inverse)
        grad_out[at] = grad
        sums_out[2:3] += jnp.sum(grad, 0, keepdims=True)
        low = grad.astype(jnp.bfloat16)
        low_out[at] = low
        units = (dot_trans(low, down[...]) * slope[at]).astype(jnp.bfloat16)
        units_out[at] = units
        wide_out[...] += jnp.sum(units.astype(jnp.float32), 0, keepdims=True)
        part_out[at] = dot_trans(units, up[...])
        return carry

    lax.fori_loop(0, 2, one, 0)


def first_body(
    grad_two, part, got, normed, inverse, gain, own, pair,
    grad_out, low_out, wide_out, own_out, sums_out,
):
    rows = part.shape[0] // 2
    sums_out[...] = jnp.zeros_like(sums_out)

    def one(block, carry):
        at = pl.ds(pl.multiple_of(block * rows, 8), rows)
        grad = grad_two[at] + (part[at] + got[at])
        sums_out[0:1] += jnp.sum(grad * normed[at], 0, keepdims=True)
        sums_out[1:2] += jnp.sum(grad, 0, keepdims=True)
        grad = norm_backward(grad * gain[...], normed[at], inverse[at])
        grad_out[at] = grad
        sums_out[2:3] += jnp.sum(grad, 0, keepdims=True)
        low = grad.astype(jnp.bfloat16)
        low_out[at] = low
        own_out[at] = dot_trans(low, own[...]).astype(jnp.bfloat16)
        turned = dot_trans(low, pair[...]).astype(jnp.bfloat16)
        wide_out[at] = turned.astype(jnp.float32) * 2.0
        return carry

    lax.fori_loop(0, 2, one, 0)


def attention_back_body(query, keys, values, sums, grads, keys_turned, query_out, keys_out, values_out):
    length = query.shape[1]
    rows = min(256, length)
    scale = 1.0 / math.sqrt(HEAD)
    key_rows, value_rows, turned = keys[0], values[0], keys_turned[0]
    key_sum = jnp.zeros((length, HEAD), jnp.float32)
    value_sum = jnp.zeros((length, HEAD), jnp.float32)
    for block in range(length // rows):
        at = pl.ds(block * rows, rows)
        asked, grad = query[0, at], grads[0, at]
        attn = jnp.exp(dot_trans(key_rows, asked) * scale - sums[0, :, at])
        value_sum += local_dot(attn.astype(jnp.bfloat16), grad)
        grad_attn = dot_trans(value_rows, grad)
        mean = jnp.sum(attn * grad_attn, 0, keepdims=True)
        scores = (attn * (grad_attn - mean)).astype(jnp.bfloat16)
        key_sum += local_dot(scores, asked)
        query_out[0, :, at] = (local_dot(turned, scores) * scale).astype(jnp.bfloat16)
    keys_out[0] = (key_sum * scale).astype(jnp.bfloat16)
    values_out[0] = value_sum.astype(jnp.bfloat16)


def pick(block, part, rows):
    return lax.dynamic_slice_in_dim(block, part * rows, rows, 0)


def widen(array):
    return array.astype(jnp.float32) * 2.0


def narrow(array):
    return (array * 0.5).astype(jnp.bfloat16)


def shards(
    mesh,
    frames,
    frame_mask,
    mask_embedding,
    query_weight,
    query_bias,
    key_weight,
    value_weight,
    value_bias,
    out_weight,
    out_bias,
    norm1_gain,
    norm1_shift,
    up_weight,
    up_bias,
    down_weight,
    down_bias,
    norm2_gain,
    norm2_shift,
    cotangent,
):
    swaps = Swaps(mesh)
    order = Order()
    clip_count, length, model_width = frames.shape
    token_rows = clip_count * length
    local_width = query_weight.shape[1]
    heads_here = local_width // HEAD
    score_scale = 1.0 / math.sqrt(HEAD)
    head_shape = (clip_count, length, heads_here, HEAD)
    own_rows = token_rows // 2
    step_rows = own_rows // STEPS
    core = swaps.core
    tensor_index = lax.axis_index("tensor")

    def step(array, k):
        return array[k * step_rows : (k + 1) * step_rows]

    out_all = lax.all_gather(widen(out_weight), "tensor", tiled=True)
    up_wide, down_wide = widen(up_weight), widen(down_weight)
    up_pair = swaps.over_core(up_wide)
    down_pair = swaps.over_core(down_wide)
    order.end(up_wide, down_wide)
    up_bias_row = up_bias.reshape(1, -1)
    up_bias_pair = swaps.over_core(up_bias_row)

    def masked(part):
        rows = pick(frame_mask.reshape(token_rows, 1), part, own_rows).astype(jnp.float32)
        block = pick(frames.reshape(token_rows, model_width), part, own_rows)
        return block.astype(jnp.float32) * (1.0 - rows) + rows * mask_embedding, rows

    masked_in, masked_rows = masked(core)
    masked_low = jnp.concatenate(
        [masked_in.astype(jnp.bfloat16), masked(1 - core)[0].astype(jnp.bfloat16)], 0
    )
    grad_out = pick(cotangent.reshape(token_rows, model_width), core, own_rows)
    masked_low = order.begin(masked_low)
    query = (local_dot(masked_low, query_weight) + query_bias).astype(jnp.bfloat16)
    keys = local_dot(masked_low, key_weight).astype(jnp.bfloat16)
    values = (local_dot(masked_low, value_weight) + value_bias).astype(jnp.bfloat16)
    query_heads = query.reshape(head_shape)
    key_heads = keys.reshape(head_shape)
    value_heads = values.reshape(head_shape)
    scores = (
        jnp.einsum("cqhd,ckhd->chqk", query_heads, key_heads, preferred_element_type=jnp.float32)
        * score_scale
    )
    row_max = jnp.max(scores, -1, keepdims=True)
    expo = jnp.exp(scores - row_max)
    totals = jnp.sum(expo, -1, keepdims=True)
    log_sum = row_max + jnp.log(totals)
    attn_low = (expo / totals).astype(jnp.bfloat16)
    context = jnp.einsum(
        "chqk,ckhd->cqhd", attn_low, value_heads, preferred_element_type=jnp.float32
    )
    context = context.reshape(token_rows, local_width).astype(jnp.bfloat16)

    narrow_half = (own_rows, local_width)
    context_send, context_own = kernel_call(
        send_body, [(narrow_half, jnp.float32)] * 2, order.begin(context)
    )
    order.end(context_send)
    context_pair = swaps.over_core(context_send)
    chip_step = (step_rows, 2 * local_width)
    *chip_steps, context_chip = kernel_call(
        pack_body,
        [(chip_step, jnp.float32)] * STEPS + [((own_rows, chip_step[1]), jnp.bfloat16)],
        *order.begin(context_own, context_pair),
    )
    order.end(*chip_steps, context_chip)
    other_wide = [swaps.over_chip(block) for block in chip_steps]
    out_all, up_pair, down_pair = order.begin(out_all, up_pair, down_pair)
    units_here = up_weight.shape[1]
    operands = (
        tensor_index.reshape(1),
        up_weight,
        up_pair,
        down_weight,
        down_pair,
        up_bias_row,
        up_bias_pair,
        out_all,
    )
    up_chip, down_chip, up_bias_chip, out_chip, out_other = kernel_call(
        join_body,
        [
            ((model_width, 2 * units_here), jnp.bfloat16),
            ((2 * units_here, model_width), jnp.bfloat16),
            ((1, 2 * units_here), jnp.float32),
            ((2 * local_width, model_width), jnp.bfloat16),
            ((2 * local_width, model_width), jnp.bfloat16),
        ],
        *operands,
        in_specs=[SMEM] + [VMEM] * 7,
    )
    out_parts = [out_chip[:local_width], out_chip[local_width:]]
    order.end(out_chip, out_other, up_chip, down_chip)

    normed_one, inverse_one, ffn_in, activ, slope = [], [], [], [], []
    hidden_one, ffn_part, ffn_got = [], [], []
    for k in range(STEPS):
        rows, wide = order.begin(step(context_chip, k), other_wide[k])
        attended = local_dot(rows, out_chip) + local_dot(narrow(wide), out_other)
        normed, inverse = normalize(step(masked_in, k) + attended + out_bias)
        hidden = normed * norm1_gain + norm1_shift
        low = hidden.astype(jnp.bfloat16)
        pre_act = local_dot(low, up_chip) + up_bias_chip
        normal_cdf = 0.5 * (1.0 + lax.erf(pre_act / math.sqrt(2.0)))
        normal_pdf = jnp.exp(-0.5 * pre_act * pre_act) / math.sqrt(2.0 * math.pi)
        units = (pre_act * normal_cdf).astype(jnp.bfloat16)
        part = order.end(local_dot(units, down_chip))
        ffn_part.append(part)
        ffn_got.append(swaps.over_chip(part))
        normed_one.append(normed)
        inverse_one.append(inverse)
        hidden_one.append(hidden)
        ffn_in.append(low)
        activ.append(units)
        slope.append(normal_cdf + pre_act * normal_pdf)

    def by_head(array):
        split = array.reshape(clip_count, length, heads_here, HEAD)
        return split.transpose(0, 2, 1, 3).reshape(clip_count * heads_here, length, HEAD)

    query, keys, values = order.begin(query, keys, values)
    keys_by_head = by_head(keys)
    attention_operands = order.end(
        by_head(query),
        keys_by_head,
        by_head(values),
        log_sum.reshape(clip_count * heads_here, 1, length),
        keys_by_head.transpose(0, 2, 1),
    )
    output, grad_h2, grad_h2_low, grad_pre, one_part, one_got = [], [], [], [], [], []
    gain_two, shift_two, bias_down, bias_up = [], [], [], []
    for k in range(STEPS):
        part, got = order.begin(ffn_part[k], ffn_got[k])
        square, wide = (step_rows, model_width), (step_rows, 2 * units_here)
        normed, grad_two, low, units, part, sums, unit_sums = kernel_call(
            second_body,
            [
                (square, jnp.float32),
                (square, jnp.float32),
                (square, jnp.bfloat16),
                (wide, jnp.bfloat16),
                (square, jnp.float32),
                ((3, model_width), jnp.float32),
                ((1, 2 * units_here), jnp.float32),
            ],
            hidden_one[k],
            part,
            got,
            step(grad_out, k),
            slope[k],
            down_chip,
            up_chip,
            down_bias[None],
            norm2_gain[None],
        )
        order.end(part)
        output.append(normed)
        gain_two.append(sums[0])
        shift_two.append(sums[1])
        bias_down.append(sums[2])
        bias_up.append(unit_sums[0])
        one_part.append(part)
        one_got.append(swaps.over_chip(part))
        grad_h2.append(grad_two)
        grad_h2_low.append(low)
        grad_pre.append(units)

    activ = jnp.concatenate(activ, 0)
    ffn_in = jnp.concatenate(ffn_in, 0)
    grad_h2_low = jnp.concatenate(grad_h2_low, 0)
    grad_pre = jnp.concatenate(grad_pre, 0)
    totals = {name: Total(swaps, order, turn) for name, turn in zip("DUT", TURNS)}
    v = {}
    heads = clip_count * heads_here
    rows = own_rows // 2

    def by_row(array):
        split = array.reshape(clip_count, heads_here, length, HEAD)
        return split.transpose(0, 2, 1, 3).reshape(token_rows, local_width)

    def weight_grad(left, right):
        return order.end(dot_rows(*order.begin(left, right)))

    def down_send():
        send = weight_grad(activ[:, units_here:], grad_h2_low)
        v["down_got"] = swaps.over_core(send)

    def down_keep():
        v["down"] = weight_grad(activ[:, :units_here], grad_h2_low)

    def up_send():
        send = weight_grad(ffn_in, grad_pre[:, units_here:])
        v["up_got"] = swaps.over_core(send)

    def up_keep():
        v["up"] = weight_grad(ffn_in, grad_pre[:, :units_here])

    def first_norm(k):
        part, got = order.begin(one_part[k], one_got[k])
        square, narrow_shape = (step_rows, model_width), (step_rows, local_width)
        v["one", k] = kernel_call(
            first_body,
            [
                (square, jnp.float32),
                (square, jnp.bfloat16),
                (narrow_shape, jnp.float32),
                (narrow_shape, jnp.bfloat16),
                ((3, model_width), jnp.float32),
            ],
            grad_h2[k],
            part,
            got,
            normed_one[k],
            inverse_one[k],
            norm1_gain[None],
            out_parts[0],
            out_parts[1],
        )
        order.end(v["one", k][2], v["one", k][3])
        if k == STEPS - 1:
            kernels = [v["one", at] for at in range(STEPS)]
            v["context_got"] = swaps.over_core(jnp.concatenate([one[2] for one in kernels], 0))
            v["context_own"] = [one[3] for one in kernels]
            v["h1_low"] = jnp.concatenate([one[1] for one in kernels], 0)
            v["h1"] = jnp.concatenate([one[0] for one in kernels], 0)

    def attention():
        grad_context = jnp.concatenate(v["context_own"] + [narrow(v["context_got"])], 0)
        head_block = pl.BlockSpec((1, length, HEAD), lambda head: (head, 0, 0))
        turned_block = pl.BlockSpec((1, HEAD, length), lambda head: (head, 0, 0))
        row_block = pl.BlockSpec((1, 1, length), lambda head: (head, 0, 0))
        operands = attention_operands[:4] + (by_head(grad_context),) + attention_operands[4:]
        grad_query, grad_keys, grad_values = kernel_call(
            attention_back_body,
            [
                ((heads, HEAD, length), jnp.bfloat16),
                ((heads, length, HEAD), jnp.bfloat16),
                ((heads, length, HEAD), jnp.bfloat16),
            ],
            *order.begin(*operands),
            grid=(heads,),
            in_specs=[head_block, head_block, head_block, row_block, head_block, turned_block],
            out_specs=[turned_block, head_block, head_block],
        )
        order.end(grad_query, grad_keys, grad_values)
        v["query"] = by_row(grad_query.transpose(0, 2, 1))
        v["values"] = by_row(grad_values)
        v["three"] = jnp.concatenate([v["query"], by_row(grad_keys), v["values"]], 1)

    attn_weight = jnp.concatenate([query_weight, key_weight, value_weight], 1)

    def terms_send():
        v["three"] = order.begin(v["three"])
        send = order.end(dot_trans(v["three"][own_rows:], attn_weight))
        v["terms_got"] = swaps.over_core(send)

    def terms_keep():
        three = order.begin(v["three"])
        v["terms"] = order.end(dot_trans(three[:own_rows], attn_weight))

    def chip_terms(k):
        at = slice(k * rows, (k + 1) * rows)
        part, got = order.begin(v["terms"][at], v["terms_got"][at])
        v["chip", k] = order.end(part + got)
        v["chip_got", k] = swaps.over_chip(v["chip", k])

    def out_send():
        send = weight_grad(context_chip[:, local_width:], v["h1_low"])
        v["out_got"] = swaps.over_core(send)

    def three_grad():
        v["three_grad"] = weight_grad(v["three"], masked_low)

    def join():
        keep, got = order.begin(
            dot_rows(context_chip[:, :local_width], v["h1_low"]), v["out_got"]
        )
        joined = order.end(jnp.concatenate([v["three_grad"], keep + got], 0))
        totals["T"].load(joined)

    def frames_step(k):
        at = slice(k * rows, (k + 1) * rows)
        part, got = order.begin(v["chip", k], v["chip_got", k])
        grad_in = v["h1"][at] + (part + got)
        v["mask", k] = jnp.sum(grad_in * masked_rows[at], 0)
        v["frames", k] = order.end(grad_in)

    def vectors():
        kernels = [v["one", at][4] for at in range(STEPS)]
        shared = (
            v["mask", 0] + v["mask", 1],
            sum(sums[2] for sums in kernels),
            sum(sums[0] for sums in kernels),
            sum(sums[1] for sums in kernels),
            sum(bias_down),
            sum(gain_two),
            sum(shift_two),
        )
        own_bias_up = sum(bias_up)
        pair = jnp.concatenate(shared + (own_bias_up[units_here:],))[None]
        mine = jnp.concatenate(shared + (own_bias_up[:units_here],))[None]
        mine, pair_got = order.begin(mine, swaps.over_core(pair))
        attention_bias = [
            jnp.sum(v[name].astype(jnp.float32), 0)[None] for name in ("query", "values")
        ]
        v["packed"] = order.end(jnp.concatenate([mine + pair_got] + attention_bias, 1))

    def vector_step(link):
        packed, got = order.begin(v["packed"], swaps.over_dp(v["packed"], link, link))
        v["packed"] = order.end(packed + got)

    stages = {
        "Ds": down_send,
        "Dk": down_keep,
        "Us": up_send,
        "Uk": up_keep,
        "N0": lambda: first_norm(0),
        "N1": lambda: first_norm(1),
        "at": attention,
        "ts": terms_send,
        "tk": terms_keep,
        "A0": lambda: chip_terms(0),
        "A1": lambda: chip_terms(1),
        "os": out_send,
        "qk": three_grad,
        "T1": join,
        "F0": lambda: frames_step(0),
        "F1": lambda: frames_step(1),
        "V": vectors,
        "V0": lambda: vector_step(0),
        "V1": lambda: vector_step(1),
        "V2": lambda: [vector_step(link) for link in range(2, len(swaps.masks))],
        "D1": lambda: totals["D"].load(v["down"], v["down_got"]),
        "U1": lambda: totals["U"].load(v["up"], v["up_got"]),
    }
    for name in ORDER:
        stages[name]() if name in stages else totals[name[0]].advance()
    frames_part = jnp.concatenate([v["frames", 0], v["frames", 1]], 0)
    frames_got = swaps.over_core(frames_part)
    output = jnp.concatenate(output, 0)
    output_got = swaps.over_core(output)
    packed = v["packed"]
    pieces = []
    start = 0
    for width in [model_width] * 7 + [units_here] + [local_width] * 2:
        pieces.append(packed[0, start : start + width])
        start += width
    (
        mask_embedding_grad,
        out_bias_grad,
        norm1_gain_grad,
        norm1_shift_grad,
        down_bias_grad,
        norm2_gain_grad,
        norm2_shift_grad,
        up_bias_grad,
        query_bias_grad,
        value_bias_grad,
    ) = pieces
    down_weight_grad, up_weight_grad, attn_weight_grad = (totals[name].finish() for name in "DUT")
    query_weight_grad, key_weight_grad, value_weight_grad, out_weight_grad = (
        attn_weight_grad[part * local_width : (part + 1) * local_width] for part in range(4)
    )
    query_weight_grad, key_weight_grad = query_weight_grad.T, key_weight_grad.T
    value_weight_grad = value_weight_grad.T

    def in_place(own, got):
        whole = jnp.stack([jnp.where(core == 0, own, got), jnp.where(core == 0, got, own)])
        return whole.reshape(token_rows, model_width)

    frames_grad = in_place(frames_part, frames_got) * (
        1.0 - frame_mask.reshape(token_rows, 1).astype(jnp.float32)
    )
    output = in_place(output, output_got) * norm2_gain + norm2_shift
    return (
        output.astype(jnp.bfloat16).reshape(frames.shape),
        frames_grad.astype(jnp.bfloat16).reshape(frames.shape),
        mask_embedding_grad,
        query_weight_grad,
        query_bias_grad,
        key_weight_grad,
        value_weight_grad,
        value_bias_grad,
        out_weight_grad,
        out_bias_grad,
        norm1_gain_grad,
        norm1_shift_grad,
        up_weight_grad,
        up_bias_grad,
        down_weight_grad,
        down_bias_grad,
        norm2_gain_grad,
        norm2_shift_grad,
    )


def solution(mesh):
    rows, columns, whole, vector = P("dp"), P(None, "tensor"), P(), P("tensor")
    return jax.shard_map(
        lambda *arrays: shards(mesh, *arrays),
        mesh=mesh,
        in_specs=(
            P("dp", None, None),
            P("dp", None),
            whole,
            columns,
            vector,
            columns,
            columns,
            vector,
            P("tensor", None),
            whole,
            whole,
            whole,
            columns,
            vector,
            P("tensor", None),
            whole,
            whole,
            whole,
            P("dp", None, None),
        ),
        out_specs=(
            P("dp", None, None),
            P("dp", None, None),
            whole,
            columns,
            vector,
            columns,
            columns,
            vector,
            P("tensor", None),
            whole,
            whole,
            whole,
            columns,
            vector,
            P("tensor", None),
            whole,
            whole,
            whole,
        ),
        check_vma=False,
    )
```

```python
import math

import jax
import jax.numpy as jnp
from jax import lax
from jax.experimental import pallas as pl
from jax.experimental.pallas import tpu as pltpu
from jax.sharding import PartitionSpec as P

HEAD = 64
AXES = ("dp", "tensor")
STEPS = 2
TURNS = (True, True, True)
ORDER = (
    "Dk", "Ds", "Uk", "N0", "Us", "D1", "U1", "N1", "D2", "U2", "at", "tk", "D3", "ts", "A0",
    "A1", "os", "qk", "U3", "T1", "F0", "D4", "T2", "D5", "F1", "U4", "T3", "V", "U5", "V0",
    "T4", "D6", "V1", "T5", "V2", "U6", "T6",
)


def local_dot(left, right):
    return jnp.dot(left, right, preferred_element_type=jnp.float32)


def dot_rows(left, right):
    return lax.dot_general(
        left, right, (((0,), (0,)), ((), ())), preferred_element_type=jnp.float32
    )


def dot_trans(left, right):
    return lax.dot_general(
        left, right, (((1,), (1,)), ((), ())), preferred_element_type=jnp.float32
    )


def normalize(values):
    centered = values - jnp.mean(values, -1, keepdims=True)
    inverse = lax.rsqrt(jnp.mean(centered * centered, -1, keepdims=True) + 1e-05)
    return (centered * inverse, inverse)


def norm_backward(grad_normed, normed, inverse):
    return inverse * (
        grad_normed
        - jnp.mean(grad_normed, -1, keepdims=True)
        - normed * jnp.mean(grad_normed * normed, -1, keepdims=True)
    )


class Swaps:
    def __init__(self, mesh):
        self.dp = mesh.shape["dp"]
        self.tensor = mesh.shape["tensor"]
        index = lax.axis_index("dp")
        self.masks = [1 << bit for bit in range(self.dp.bit_length() - 1)]
        self.coords = [(index >> bit) & 1 for bit in range(len(self.masks))]
        self.core = lax.axis_index("tensor") % 2

    def move(self, value, target):
        pairs = []
        for row in range(self.dp):
            for column in range(self.tensor):
                to_row, to_column = target(row, column)
                pairs.append((row * self.tensor + column, to_row * self.tensor + to_column))
        return lax.ppermute(value, AXES, pairs)

    def over_core(self, value):
        return self.move(value, lambda row, column: (row, column ^ 1))

    def over_chip(self, value):
        return self.move(value, lambda row, column: (row, column ^ 2))

    def over_dp(self, value, even, odd):
        masks = self.masks
        return self.move(
            value, lambda row, column: (row ^ masks[odd if column % 2 else even], column)
        )

    def plan(self, turn):
        steps = list(range(len(self.masks)))
        turned = steps[1::-1] + steps[2:] if turn else steps
        result = []
        for even, odd in zip(steps, turned):
            coord = jnp.where(self.core == 0, self.coords[even], self.coords[odd])
            result.append((even, odd, coord))
        return result


class Order:
    def __init__(self):
        self.last = ()

    def begin(self, *arrays):
        arrays, _ = lax.optimization_barrier((arrays, self.last))
        self.last = ()
        return arrays[0] if len(arrays) == 1 else arrays

    def end(self, *arrays):
        self.last += arrays
        return arrays[0] if len(arrays) == 1 else arrays


class Total:
    def __init__(self, swaps, order, turn):
        self.swaps, self.order, self.plan = swaps, order, swaps.plan(turn)
        self.queue = [self.first] + [self.halve] * (len(self.plan) - 2)
        self.queue += [self.exchange, self.settle] + [self.double] * (len(self.plan) - 1)

    def load(self, value, got=None):
        self.keep, self.got, self.at = value, got, -1
        self.queue.pop(0) if got is None else None
        if got is None:
            self.first()
        else:
            self.queue[0] = self.halve
            self.advance()

    def advance(self, count=1):
        for _ in range(count):
            if self.queue:
                self.queue.pop(0)()

    def send(self, value):
        even, odd, _ = self.plan[self.at]
        self.got = self.swaps.over_dp(value, even, odd)

    def first(self):
        self.at = 0
        coord = self.plan[0][2]
        rows = self.keep.shape[0] // 2
        value = self.order.begin(self.keep)
        self.send(self.order.end(pick(value, 1 - coord, rows)))
        self.keep = pick(value, coord, rows)

    def halve(self):
        self.at += 1
        coord = self.plan[self.at][2]
        rows = self.keep.shape[0] // 2
        keep, got = self.order.begin(self.keep, self.got)
        send = pick(keep, 1 - coord, rows) + pick(got, 1 - coord, rows)
        self.keep = pick(keep, coord, rows) + pick(got, coord, rows)
        self.order.end(send, self.keep)
        self.send(send)

    def exchange(self):
        self.at += 1
        keep, got = self.order.begin(self.keep, self.got)
        self.keep = self.order.end(keep + got)
        self.send(self.keep)

    def settle(self):
        keep, got = self.order.begin(self.keep, self.got)
        self.keep = self.order.end(keep + got)
        self.at -= 1
        self.send(self.keep)

    def double(self):
        first = self.plan[self.at][2] == 0
        keep, got = self.order.begin(self.keep, self.got)
        self.keep = self.order.end(
            jnp.concatenate([jnp.where(first, keep, got), jnp.where(first, got, keep)], 0)
        )
        self.at -= 1
        if self.at >= 0:
            self.send(self.keep)

    def finish(self):
        self.advance(len(self.queue))
        return self.keep


VMEM = pl.BlockSpec(memory_space=pltpu.VMEM)
SMEM = pl.BlockSpec(memory_space=pltpu.SMEM)


def kernel_call(body, outputs, *arrays, **options):
    shapes = [jax.ShapeDtypeStruct(shape, kind) for shape, kind in outputs]
    options.setdefault("in_specs", [VMEM] * len(arrays))
    options.setdefault("out_specs", [VMEM] * len(shapes))
    return pl.pallas_call(
        body,
        out_shape=shapes,
        cost_estimate=pl.CostEstimate(flops=1, bytes_accessed=1, transcendentals=0),
        compiler_params=pltpu.CompilerParams(vmem_limit_bytes=24 * 1024 * 1024),
        **options,
    )(*arrays)


def send_body(context, send_out, own_out):
    rows = send_out.shape[0]
    send_out[...] = context[rows:].astype(jnp.float32) * 2.0
    own_out[...] = context[:rows].astype(jnp.float32) * 2.0


def pack_body(own, pair, *outs):
    *steps, chip_out = outs
    rows, width = steps[0].shape[0], own.shape[1]
    for index, out in enumerate(steps):
        at = slice(index * rows, (index + 1) * rows)
        out[:, :width] = own[at]
        out[:, width:] = pair[at]
        chip_out[at, :width] = (own[at] * 0.5).astype(jnp.bfloat16)
        chip_out[at, width:] = (pair[at] * 0.5).astype(jnp.bfloat16)


def join_body(
    index, up, up_pair, down, down_pair, bias, bias_pair, out_all,
    up_out, down_out, bias_out, chip_out, other_out,
):
    width = up.shape[1]
    up_out[:, :width] = up[...]
    up_out[:, width:] = (up_pair[...] * 0.5).astype(jnp.bfloat16)
    down_out[:width] = down[...]
    down_out[width:] = (down_pair[...] * 0.5).astype(jnp.bfloat16)
    bias_out[:, :width] = bias[...]
    bias_out[:, width:] = bias_pair[...]
    rows = chip_out.shape[0] // 2
    for mask, out in enumerate((chip_out, chip_out, other_out, other_out)):
        at = pl.ds(pl.multiple_of((index[0] ^ mask) * rows, 8), rows)
        to = slice(mask % 2 * rows, (mask % 2 + 1) * rows)
        out[to] = (out_all[at] * 0.5).astype(jnp.bfloat16)


def second_body(
    hidden, part, got, cotangent, slope, down, up, bias, gain,
    normed_out, grad_out, low_out, units_out, part_out, sums_out, wide_out,
):
    rows = hidden.shape[0] // 2
    sums_out[...] = jnp.zeros_like(sums_out)
    wide_out[...] = jnp.zeros_like(wide_out)

    def one(block, carry):
        at = pl.ds(pl.multiple_of(block * rows, 8), rows)
        normed, inverse = normalize(hidden[at] + (part[at] + got[at]) + bias[...])
        normed_out[at] = normed
        grad = cotangent[at].astype(jnp.float32)
        sums_out[0:1] += jnp.sum(grad * normed, 0, keepdims=True)
        sums_out[1:2] += jnp.sum(grad, 0, keepdims=True)
        grad = norm_backward(grad * gain[...], normed, inverse)
        grad_out[at] = grad
        sums_out[2:3] += jnp.sum(grad, 0, keepdims=True)
        low = grad.astype(jnp.bfloat16)
        low_out[at] = low
        units = (dot_trans(low, down[...]) * slope[at]).astype(jnp.bfloat16)
        units_out[at] = units
        wide_out[...] += jnp.sum(units.astype(jnp.float32), 0, keepdims=True)
        part_out[at] = dot_trans(units, up[...])
        return carry

    lax.fori_loop(0, 2, one, 0)


def first_body(
    grad_two, part, got, normed, inverse, gain, own, pair,
    grad_out, low_out, wide_out, own_out, sums_out,
):
    rows = part.shape[0] // 2
    sums_out[...] = jnp.zeros_like(sums_out)

    def one(block, carry):
        at = pl.ds(pl.multiple_of(block * rows, 8), rows)
        grad = grad_two[at] + (part[at] + got[at])
        sums_out[0:1] += jnp.sum(grad * normed[at], 0, keepdims=True)
        sums_out[1:2] += jnp.sum(grad, 0, keepdims=True)
        grad = norm_backward(grad * gain[...], normed[at], inverse[at])
        grad_out[at] = grad
        sums_out[2:3] += jnp.sum(grad, 0, keepdims=True)
        low = grad.astype(jnp.bfloat16)
        low_out[at] = low
        own_out[at] = dot_trans(low, own[...]).astype(jnp.bfloat16)
        turned = dot_trans(low, pair[...]).astype(jnp.bfloat16)
        wide_out[at] = turned.astype(jnp.float32) * 2.0
        return carry

    lax.fori_loop(0, 2, one, 0)


def attention_back_body(query, keys, values, sums, grads, keys_turned, query_out, keys_out, values_out):
    length = query.shape[1]
    rows = min(256, length)
    scale = 1.0 / math.sqrt(HEAD)
    key_rows, value_rows, turned = keys[0], values[0], keys_turned[0]
    key_sum = jnp.zeros((length, HEAD), jnp.float32)
    value_sum = jnp.zeros((length, HEAD), jnp.float32)
    for block in range(length // rows):
        at = pl.ds(block * rows, rows)
        asked, grad = query[0, at], grads[0, at]
        attn = jnp.exp(dot_trans(key_rows, asked) * scale - sums[0, :, at])
        value_sum += local_dot(attn.astype(jnp.bfloat16), grad)
        grad_attn = dot_trans(value_rows, grad)
        mean = jnp.sum(attn * grad_attn, 0, keepdims=True)
        scores = (attn * (grad_attn - mean)).astype(jnp.bfloat16)
        key_sum += local_dot(scores, asked)
        query_out[0, :, at] = (local_dot(turned, scores) * scale).astype(jnp.bfloat16)
    keys_out[0] = (key_sum * scale).astype(jnp.bfloat16)
    values_out[0] = value_sum.astype(jnp.bfloat16)


def pick(block, part, rows):
    return lax.dynamic_slice_in_dim(block, part * rows, rows, 0)


def widen(array):
    return array.astype(jnp.float32) * 2.0


def narrow(array):
    return (array * 0.5).astype(jnp.bfloat16)


def shards(
    mesh,
    frames,
    frame_mask,
    mask_embedding,
    query_weight,
    query_bias,
    key_weight,
    value_weight,
    value_bias,
    out_weight,
    out_bias,
    norm1_gain,
    norm1_shift,
    up_weight,
    up_bias,
    down_weight,
    down_bias,
    norm2_gain,
    norm2_shift,
    cotangent,
):
    swaps = Swaps(mesh)
    order = Order()
    clip_count, length, model_width = frames.shape
    token_rows = clip_count * length
    local_width = query_weight.shape[1]
    heads_here = local_width // HEAD
    score_scale = 1.0 / math.sqrt(HEAD)
    head_shape = (clip_count, length, heads_here, HEAD)
    own_rows = token_rows // 2
    step_rows = own_rows // STEPS
    core = swaps.core
    tensor_index = lax.axis_index("tensor")

    def step(array, k):
        return array[k * step_rows : (k + 1) * step_rows]

    out_all = lax.all_gather(widen(out_weight), "tensor", tiled=True)
    up_wide, down_wide = widen(up_weight), widen(down_weight)
    up_pair = swaps.over_core(up_wide)
    down_pair = swaps.over_core(down_wide)
    order.end(up_wide, down_wide)
    up_bias_row = up_bias.reshape(1, -1)
    up_bias_pair = swaps.over_core(up_bias_row)

    def masked(part):
        rows = pick(frame_mask.reshape(token_rows, 1), part, own_rows).astype(jnp.float32)
        block = pick(frames.reshape(token_rows, model_width), part, own_rows)
        return block.astype(jnp.float32) * (1.0 - rows) + rows * mask_embedding, rows

    masked_in, masked_rows = masked(core)
    masked_low = jnp.concatenate(
        [masked_in.astype(jnp.bfloat16), masked(1 - core)[0].astype(jnp.bfloat16)], 0
    )
    grad_out = pick(cotangent.reshape(token_rows, model_width), core, own_rows)
    masked_low = order.begin(masked_low)
    query = (local_dot(masked_low, query_weight) + query_bias).astype(jnp.bfloat16)
    keys = local_dot(masked_low, key_weight).astype(jnp.bfloat16)
    values = (local_dot(masked_low, value_weight) + value_bias).astype(jnp.bfloat16)
    query_heads = query.reshape(head_shape)
    key_heads = keys.reshape(head_shape)
    value_heads = values.reshape(head_shape)
    scores = (
        jnp.einsum("cqhd,ckhd->chqk", query_heads, key_heads, preferred_element_type=jnp.float32)
        * score_scale
    )
    row_max = jnp.max(scores, -1, keepdims=True)
    expo = jnp.exp(scores - row_max)
    totals = jnp.sum(expo, -1, keepdims=True)
    log_sum = row_max + jnp.log(totals)
    attn_low = (expo / totals).astype(jnp.bfloat16)
    context = jnp.einsum(
        "chqk,ckhd->cqhd", attn_low, value_heads, preferred_element_type=jnp.float32
    )
    context = context.reshape(token_rows, local_width).astype(jnp.bfloat16)

    narrow_half = (own_rows, local_width)
    context_send, context_own = kernel_call(
        send_body, [(narrow_half, jnp.float32)] * 2, order.begin(context)
    )
    order.end(context_send)
    context_pair = swaps.over_core(context_send)
    chip_step = (step_rows, 2 * local_width)
    *chip_steps, context_chip = kernel_call(
        pack_body,
        [(chip_step, jnp.float32)] * STEPS + [((own_rows, chip_step[1]), jnp.bfloat16)],
        *order.begin(context_own, context_pair),
    )
    order.end(*chip_steps, context_chip)
    other_wide = [swaps.over_chip(block) for block in chip_steps]
    out_all, up_pair, down_pair = order.begin(out_all, up_pair, down_pair)
    units_here = up_weight.shape[1]
    operands = (
        tensor_index.reshape(1),
        up_weight,
        up_pair,
        down_weight,
        down_pair,
        up_bias_row,
        up_bias_pair,
        out_all,
    )
    up_chip, down_chip, up_bias_chip, out_chip, out_other = kernel_call(
        join_body,
        [
            ((model_width, 2 * units_here), jnp.bfloat16),
            ((2 * units_here, model_width), jnp.bfloat16),
            ((1, 2 * units_here), jnp.float32),
            ((2 * local_width, model_width), jnp.bfloat16),
            ((2 * local_width, model_width), jnp.bfloat16),
        ],
        *operands,
        in_specs=[SMEM] + [VMEM] * 7,
    )
    out_parts = [out_chip[:local_width], out_chip[local_width:]]
    order.end(out_chip, out_other, up_chip, down_chip)

    normed_one, inverse_one, ffn_in, activ, slope = [], [], [], [], []
    hidden_one, ffn_part, ffn_got = [], [], []
    for k in range(STEPS):
        rows, wide = order.begin(step(context_chip, k), other_wide[k])
        attended = local_dot(rows, out_chip) + local_dot(narrow(wide), out_other)
        normed, inverse = normalize(step(masked_in, k) + attended + out_bias)
        hidden = normed * norm1_gain + norm1_shift
        low = hidden.astype(jnp.bfloat16)
        pre_act = local_dot(low, up_chip) + up_bias_chip
        normal_cdf = 0.5 * (1.0 + lax.erf(pre_act / math.sqrt(2.0)))
        normal_pdf = jnp.exp(-0.5 * pre_act * pre_act) / math.sqrt(2.0 * math.pi)
        units = (pre_act * normal_cdf).astype(jnp.bfloat16)
        part = order.end(local_dot(units, down_chip))
        ffn_part.append(part)
        ffn_got.append(swaps.over_chip(part))
        normed_one.append(normed)
        inverse_one.append(inverse)
        hidden_one.append(hidden)
        ffn_in.append(low)
        activ.append(units)
        slope.append(normal_cdf + pre_act * normal_pdf)

    def by_head(array):
        split = array.reshape(clip_count, length, heads_here, HEAD)
        return split.transpose(0, 2, 1, 3).reshape(clip_count * heads_here, length, HEAD)

    query, keys, values = order.begin(query, keys, values)
    keys_by_head = by_head(keys)
    attention_operands = order.end(
        by_head(query),
        keys_by_head,
        by_head(values),
        log_sum.reshape(clip_count * heads_here, 1, length),
        keys_by_head.transpose(0, 2, 1),
    )
    output, grad_h2, grad_h2_low, grad_pre, one_part, one_got = [], [], [], [], [], []
    gain_two, shift_two, bias_down, bias_up = [], [], [], []
    for k in range(STEPS):
        part, got = order.begin(ffn_part[k], ffn_got[k])
        square, wide = (step_rows, model_width), (step_rows, 2 * units_here)
        normed, grad_two, low, units, part, sums, unit_sums = kernel_call(
            second_body,
            [
                (square, jnp.float32),
                (square, jnp.float32),
                (square, jnp.bfloat16),
                (wide, jnp.bfloat16),
                (square, jnp.float32),
                ((3, model_width), jnp.float32),
                ((1, 2 * units_here), jnp.float32),
            ],
            hidden_one[k],
            part,
            got,
            step(grad_out, k),
            slope[k],
            down_chip,
            up_chip,
            down_bias[None],
            norm2_gain[None],
        )
        order.end(part)
        output.append(normed)
        gain_two.append(sums[0])
        shift_two.append(sums[1])
        bias_down.append(sums[2])
        bias_up.append(unit_sums[0])
        one_part.append(part)
        one_got.append(swaps.over_chip(part))
        grad_h2.append(grad_two)
        grad_h2_low.append(low)
        grad_pre.append(units)

    activ = jnp.concatenate(activ, 0)
    ffn_in = jnp.concatenate(ffn_in, 0)
    grad_h2_low = jnp.concatenate(grad_h2_low, 0)
    grad_pre = jnp.concatenate(grad_pre, 0)
    totals = {name: Total(swaps, order, turn) for name, turn in zip("DUT", TURNS)}
    v = {}
    heads = clip_count * heads_here
    rows = own_rows // 2

    def by_row(array):
        split = array.reshape(clip_count, heads_here, length, HEAD)
        return split.transpose(0, 2, 1, 3).reshape(token_rows, local_width)

    def weight_grad(left, right):
        return order.end(dot_rows(*order.begin(left, right)))

    def down_send():
        send = weight_grad(activ[:, units_here:], grad_h2_low)
        v["down_got"] = swaps.over_core(send)

    def down_keep():
        v["down"] = weight_grad(activ[:, :units_here], grad_h2_low)

    def up_send():
        send = weight_grad(ffn_in, grad_pre[:, units_here:])
        v["up_got"] = swaps.over_core(send)

    def up_keep():
        v["up"] = weight_grad(ffn_in, grad_pre[:, :units_here])

    def first_norm(k):
        part, got = order.begin(one_part[k], one_got[k])
        square, narrow_shape = (step_rows, model_width), (step_rows, local_width)
        v["one", k] = kernel_call(
            first_body,
            [
                (square, jnp.float32),
                (square, jnp.bfloat16),
                (narrow_shape, jnp.float32),
                (narrow_shape, jnp.bfloat16),
                ((3, model_width), jnp.float32),
            ],
            grad_h2[k],
            part,
            got,
            normed_one[k],
            inverse_one[k],
            norm1_gain[None],
            out_parts[0],
            out_parts[1],
        )
        order.end(v["one", k][2], v["one", k][3])
        if k == STEPS - 1:
            kernels = [v["one", at] for at in range(STEPS)]
            v["context_got"] = swaps.over_core(jnp.concatenate([one[2] for one in kernels], 0))
            v["context_own"] = [one[3] for one in kernels]
            v["h1_low"] = jnp.concatenate([one[1] for one in kernels], 0)
            v["h1"] = jnp.concatenate([one[0] for one in kernels], 0)

    def attention():
        grad_context = jnp.concatenate(v["context_own"] + [narrow(v["context_got"])], 0)
        head_block = pl.BlockSpec((1, length, HEAD), lambda head: (head, 0, 0))
        turned_block = pl.BlockSpec((1, HEAD, length), lambda head: (head, 0, 0))
        row_block = pl.BlockSpec((1, 1, length), lambda head: (head, 0, 0))
        operands = attention_operands[:4] + (by_head(grad_context),) + attention_operands[4:]
        grad_query, grad_keys, grad_values = kernel_call(
            attention_back_body,
            [
                ((heads, HEAD, length), jnp.bfloat16),
                ((heads, length, HEAD), jnp.bfloat16),
                ((heads, length, HEAD), jnp.bfloat16),
            ],
            *order.begin(*operands),
            grid=(heads,),
            in_specs=[head_block, head_block, head_block, row_block, head_block, turned_block],
            out_specs=[turned_block, head_block, head_block],
        )
        order.end(grad_query, grad_keys, grad_values)
        v["query"] = by_row(grad_query.transpose(0, 2, 1))
        v["values"] = by_row(grad_values)
        v["three"] = jnp.concatenate([v["query"], by_row(grad_keys), v["values"]], 1)

    attn_weight = jnp.concatenate([query_weight, key_weight, value_weight], 1)

    def terms_send():
        v["three"] = order.begin(v["three"])
        send = order.end(dot_trans(v["three"][own_rows:], attn_weight))
        v["terms_got"] = swaps.over_core(send)

    def terms_keep():
        three = order.begin(v["three"])
        v["terms"] = order.end(dot_trans(three[:own_rows], attn_weight))

    def chip_terms(k):
        at = slice(k * rows, (k + 1) * rows)
        part, got = order.begin(v["terms"][at], v["terms_got"][at])
        v["chip", k] = order.end(part + got)
        v["chip_got", k] = swaps.over_chip(v["chip", k])

    def out_send():
        send = weight_grad(context_chip[:, local_width:], v["h1_low"])
        v["out_got"] = swaps.over_core(send)

    def three_grad():
        v["three_grad"] = weight_grad(v["three"], masked_low)

    def join():
        keep, got = order.begin(
            dot_rows(context_chip[:, :local_width], v["h1_low"]), v["out_got"]
        )
        joined = order.end(jnp.concatenate([v["three_grad"], keep + got], 0))
        totals["T"].load(joined)

    def frames_step(k):
        at = slice(k * rows, (k + 1) * rows)
        part, got = order.begin(v["chip", k], v["chip_got", k])
        grad_in = v["h1"][at] + (part + got)
        v["mask", k] = jnp.sum(grad_in * masked_rows[at], 0)
        v["frames", k] = order.end(grad_in)

    def vectors():
        kernels = [v["one", at][4] for at in range(STEPS)]
        shared = (
            v["mask", 0] + v["mask", 1],
            sum(sums[2] for sums in kernels),
            sum(sums[0] for sums in kernels),
            sum(sums[1] for sums in kernels),
            sum(bias_down),
            sum(gain_two),
            sum(shift_two),
        )
        own_bias_up = sum(bias_up)
        pair = jnp.concatenate(shared + (own_bias_up[units_here:],))[None]
        mine = jnp.concatenate(shared + (own_bias_up[:units_here],))[None]
        mine, pair_got = order.begin(mine, swaps.over_core(pair))
        attention_bias = [
            jnp.sum(v[name].astype(jnp.float32), 0)[None] for name in ("query", "values")
        ]
        v["packed"] = order.end(jnp.concatenate([mine + pair_got] + attention_bias, 1))

    def vector_step(link):
        packed, got = order.begin(v["packed"], swaps.over_dp(v["packed"], link, link))
        v["packed"] = order.end(packed + got)

    stages = {
        "Ds": down_send,
        "Dk": down_keep,
        "Us": up_send,
        "Uk": up_keep,
        "N0": lambda: first_norm(0),
        "N1": lambda: first_norm(1),
        "at": attention,
        "ts": terms_send,
        "tk": terms_keep,
        "A0": lambda: chip_terms(0),
        "A1": lambda: chip_terms(1),
        "os": out_send,
        "qk": three_grad,
        "T1": join,
        "F0": lambda: frames_step(0),
        "F1": lambda: frames_step(1),
        "V": vectors,
        "V0": lambda: vector_step(0),
        "V1": lambda: vector_step(1),
        "V2": lambda: [vector_step(link) for link in range(2, len(swaps.masks))],
        "D1": lambda: totals["D"].load(v["down"], v["down_got"]),
        "U1": lambda: totals["U"].load(v["up"], v["up_got"]),
    }
    for name in ORDER:
        stages[name]() if name in stages else totals[name[0]].advance()
    frames_part = jnp.concatenate([v["frames", 0], v["frames", 1]], 0)
    frames_got = swaps.over_core(frames_part)
    output = jnp.concatenate(output, 0)
    output_got = swaps.over_core(output)
    packed = v["packed"]
    pieces = []
    start = 0
    for width in [model_width] * 7 + [units_here] + [local_width] * 2:
        pieces.append(packed[0, start : start + width])
        start += width
    (
        mask_embedding_grad,
        out_bias_grad,
        norm1_gain_grad,
        norm1_shift_grad,
        down_bias_grad,
        norm2_gain_grad,
        norm2_shift_grad,
        up_bias_grad,
        query_bias_grad,
        value_bias_grad,
    ) = pieces
    down_weight_grad, up_weight_grad, attn_weight_grad = (totals[name].finish() for name in "DUT")
    query_weight_grad, key_weight_grad, value_weight_grad, out_weight_grad = (
        attn_weight_grad[part * local_width : (part + 1) * local_width] for part in range(4)
    )
    query_weight_grad, key_weight_grad = query_weight_grad.T, key_weight_grad.T
    value_weight_grad = value_weight_grad.T

    def in_place(own, got):
        whole = jnp.stack([jnp.where(core == 0, own, got), jnp.where(core == 0, got, own)])
        return whole.reshape(token_rows, model_width)

    frames_grad = in_place(frames_part, frames_got) * (
        1.0 - frame_mask.reshape(token_rows, 1).astype(jnp.float32)
    )
    output = in_place(output, output_got) * norm2_gain + norm2_shift
    return (
        output.astype(jnp.bfloat16).reshape(frames.shape),
        frames_grad.astype(jnp.bfloat16).reshape(frames.shape),
        mask_embedding_grad,
        query_weight_grad,
        query_bias_grad,
        key_weight_grad,
        value_weight_grad,
        value_bias_grad,
        out_weight_grad,
        out_bias_grad,
        norm1_gain_grad,
        norm1_shift_grad,
        up_weight_grad,
        up_bias_grad,
        down_weight_grad,
        down_bias_grad,
        norm2_gain_grad,
        norm2_shift_grad,
    )


def solution(mesh):
    rows, columns, whole, vector = P("dp"), P(None, "tensor"), P(), P("tensor")
    return jax.shard_map(
        lambda *arrays: shards(mesh, *arrays),
        mesh=mesh,
        in_specs=(
            P("dp", None, None),
            P("dp", None),
            whole,
            columns,
            vector,
            columns,
            columns,
            vector,
            P("tensor", None),
            whole,
            whole,
            whole,
            columns,
            vector,
            P("tensor", None),
            whole,
            whole,
            whole,
            P("dp", None, None),
        ),
        out_specs=(
            P("dp", None, None),
            P("dp", None, None),
            whole,
            columns,
            vector,
            columns,
            columns,
            vector,
            P("tensor", None),
            whole,
            whole,
            whole,
            columns,
            vector,
            P("tensor", None),
            whole,
            whole,
            whole,
        ),
        check_vma=False,
    )
```
